768 devices in a mesh: tm: 96 (over z_lo, y, core), space: 8 (over z_hi, x).
Axes of the slice: x: 4, y: 8, z: 12 (z_hi: 2, z_lo: 6; z = z_hi * 6 + z_lo), core: 2. Of those that a mesh axis runs over, the one named last changes fastest.
Arguments:
- eigvecs: bfloat16 [2, 3, 96, 4096, 256], P(None, None, 'tm', 'space'), may hold values from -0.09375 to 0.09375
- propagator: bfloat16 [2, 3, 96, 4096, 128], P(None, None, 'tm', 'space'), may hold values from -6 to 6
- elementals: bfloat16 [96, 8, 2, 256, 256], P('tm'), may hold values from -0.0017089844 to 0.0017089844
- sink_times: int32 [96, 16], P('tm'), may hold values from 0 to 95, as said below
- momenta: int32 [96, 16], P('tm'), may hold values from 0 to 7
Outputs:
- traces: float32 [2, 96, 16], P(None, 'tm')
The draws below stay inside these ranges and needn't reach their ends.
Inputs may be any that keep to these rules, and one draw needn't show every extreme that they name: (sink_times[t, k] - t) modulo 96 lies in 0 to 49 or equals 95; item 0 of every slice t has sink time (t + 48) modulo 96, item 1 has (t - 1) modulo 96.
All inputs are finite; a program needn't handle non-finite values.
Results may differ from the reference program's by a relative error of at most 0.0049.
Values may be sent and summed in bfloat16 or wider, within the bound.
A program may use at most 32 MiB of HBM per device.

```python
import jax
import jax.numpy as jnp
from jax import lax

NVEC = 256
NC = 3
NMOM = 8
ITEMS_DEV = 16
SB = 128
NT = 96
SITES = 4096


def draw_sink_times(key, part):
    separation = jax.random.randint(jax.random.fold_in(key, 17), (NT, ITEMS_DEV), -1, NT // 2 + 2, dtype=jnp.int32)
    separation = separation.at[:, 0].set(NT // 2)
    separation = separation.at[:, 1].set(-1)
    anchor = jnp.arange(NT, dtype=jnp.int32)[:, None]
    return ((anchor + separation + NT) % NT).astype(jnp.int32)


def with_ends(drawn, stream_key, least, top_value):
    index_at = [jax.random.randint(jax.random.fold_in(stream_key, axis), (), 0, length) for axis, length in enumerate(drawn.shape)]
    widest = drawn.shape.index(max(drawn.shape))
    neighbour = index_at[:widest] + [(index_at[widest] + 1) % drawn.shape[widest]] + index_at[widest + 1:]
    return drawn.at[tuple(index_at)].set(least).at[tuple(neighbour)].set(top_value)


def block_levels(stream_key, dims, pieces, low, high):
    def one(dim, shards_of):
        draws = jax.random.uniform(jax.random.fold_in(jax.random.fold_in(stream_key, 6), dim), (shards_of,), jnp.float32, low / len(pieces), high / len(pieces))
        return jnp.repeat(jnp.exp(draws), dims[dim] // shards_of).reshape((-1,) + (1,) * (len(dims) - dim - 1))

    factor_of = one(*pieces[0])
    for cut in pieces[1:]:
        factor_of = factor_of * one(*cut)
    return factor_of


def centred(own_key, extent, deviation, bound, cuts=(), held_as=jnp.bfloat16):
    values = jax.random.normal(own_key, extent, jnp.float32) * deviation
    if len(cuts) > 0:
        values = block_levels(own_key, extent, cuts, -0.22, 0.18) * values
    return jnp.clip(values, min=-bound, max=bound).astype(held_as)


def setup_inputs(seed: int = 0) -> dict:
    splits = jax.random.split(jax.random.key(seed), 6)
    return {
        "eigvecs": centred(splits[0], (2, NC, NT, SITES, NVEC), ((6 * SITES) ** -0.5), 0.09375, ((2, 96), (3, 8))),
        "propagator": centred(splits[1], (2, NC, NT, SITES, SB), 1.0, 6.0, ((2, 96), (3, 8))),
        "elementals": centred(splits[2], (NT, NMOM, 2, NVEC, NVEC), (0.35 / (NVEC * SB ** 0.5)), 0.0017089844, ((0, 96),)),
        "sink_times": draw_sink_times(jax.random.fold_in(splits[5], 71), 0),
        "momenta": with_ends(jax.random.randint(splits[4], (NT, ITEMS_DEV), 0, NMOM), jax.random.fold_in(splits[4], 1), 0, NMOM - 1).astype(jnp.int32),
    }


def project(index, eigvecs, propagator):
    vecs = lax.dynamic_index_in_dim(eigvecs, index, 2, keepdims=False).reshape(2, -1, NVEC)
    props = lax.dynamic_index_in_dim(propagator, index, 2, keepdims=False).reshape(2, -1, SB)
    real_part = jnp.dot(props[0].T, vecs[0], preferred_element_type=jnp.float32) + jnp.dot(props[1].T, vecs[1], preferred_element_type=jnp.float32)
    imag_part = jnp.dot(props[1].T, vecs[0], preferred_element_type=jnp.float32) - jnp.dot(props[0].T, vecs[1], preferred_element_type=jnp.float32)
    return jnp.stack([real_part, imag_part], axis=1).astype(jnp.bfloat16)


def reference(eigvecs, propagator, elementals, sink_times, momenta):
    perams = lax.map(lambda index: project(index, eigvecs, propagator), jnp.arange(NT, dtype=jnp.int32))
    flat_perams = perams.reshape(NT, -1)

    def contract(index):
        moments = elementals[index].astype(jnp.float32)
        tau_block = perams[index].astype(jnp.float32)
        expand = jnp.einsum("prab,sqb->prsqa", moments, tau_block)
        real_part = expand[:, 0, :, 0] - expand[:, 1, :, 1]
        imag_part = expand[:, 0, :, 1] + expand[:, 1, :, 0]
        mixed_terms = jnp.stack([real_part, imag_part], axis=2).astype(jnp.bfloat16)
        swapped = jnp.stack([mixed_terms[:, :, 1], -mixed_terms[:, :, 0]], axis=2)
        weights = jnp.stack([mixed_terms, swapped], axis=1).reshape(2 * NMOM, -1)
        tables = jnp.dot(weights, flat_perams.T, preferred_element_type=jnp.float32).reshape(NMOM, 2, NT)
        picked = tables[momenta[index], :, sink_times[index]]
        return picked.T

    result = lax.map(contract, jnp.arange(NT, dtype=jnp.int32))
    return jnp.transpose(result, (1, 0, 2))
```

```python
import functools

import jax
import jax.numpy as jnp
from jax import lax
from jax.experimental import pallas as pl
from jax.experimental.pallas import tpu as pltpu
from jax.sharding import PartitionSpec as P

X, Y, ZL, CORES = 4, 8, 6, 2
ZR = 2 * ZL
OFFSETS = (6, 7, 1, 8, 2, 9, 3)
F32 = jnp.float32
BF16 = jnp.bfloat16


def kernel(
    vec_hbm, prop_hbm, elem_hbm, sink_hbm, mom_hbm, out_ref,
    vec, prop, elem, xsend, xrecv, zsend, zrecv, gath, mix, sink, mom, rows, ranks,
    load_sem, elem_sem, item_sem, item_send, item_recv,
    xs_sem, xr_sem, zs_sem, zr_sem, ys_sem, yr_sem, mix_sem, fs_sem, fr_sem,
):
    tm, space = lax.axis_index("tm"), lax.axis_index("space")
    core, chip = lax.rem(tm, 2), lax.div(tm, 2)
    y, c = lax.rem(chip, Y), lax.div(chip, Y)
    h, x = lax.div(space, X), lax.rem(space, X)
    ring = h * ZL + c
    columns = prop.shape[-1]
    wide = columns // X
    narrow = wide // 2

    def device(xx, yy, zz, kk):
        hh, cc = lax.div(zz, ZL), lax.rem(zz, ZL)
        return {"tm": (cc * Y + yy) * 2 + kk, "space": hh * X + xx}

    def send(src, dst, ssem, rsem, where):
        return pltpu.make_async_remote_copy(
            src_ref=src, dst_ref=dst, send_sem=ssem, recv_sem=rsem,
            device_id=where, device_id_type=pl.DeviceIdType.MESH,
        )

    far = lax.rem(ring + ZL, ZR)
    special = jnp.logical_or(
        jnp.logical_and(y == 0, core == 0), jnp.logical_and(y == Y - 1, core == 1)
    )
    final = [
        (dx, dz, dk) for dz in range(2) for dx in range(X) for dk in range(2) if dx or dz or dk
    ]

    def final_device(dx, dz, dk):
        return device(
            lax.rem(x + dx, X), y, far if dz else ring, (1 - core) if dk else core
        )

    loads = []
    for q in range(2):
        for col in range(3):
            a = pltpu.make_async_copy(vec_hbm.at[q, col, 0], vec.at[q, col], load_sem.at[0, q, col])
            b = pltpu.make_async_copy(prop_hbm.at[q, col, 0], prop.at[q, col], load_sem.at[1, q, col])
            a.start()
            b.start()
            loads.append((a, b))
    elem_load = pltpu.make_async_copy(elem_hbm.at[0], elem, elem_sem)
    elem_load.start()
    own_items = [
        pltpu.make_async_copy(sink_hbm, sink.at[pl.ds(core, 1)], item_sem.at[0]),
        pltpu.make_async_copy(mom_hbm, mom.at[pl.ds(core, 1)], item_sem.at[1]),
    ]
    for copy in own_items:
        copy.start()

    barrier = pltpu.get_barrier_semaphore()
    partners = [final_device(*d) for d in final]
    partners += [device(x, lax.rem(y + r, Y), ring, core) for r in range(1, Y)]
    partners += [device(x, y, lax.rem(ring + r, ZR), core) for r in range(1, ZR) if r != ZL]
    for where in partners:
        pl.semaphore_signal(barrier, inc=1, device_id=where, device_id_type=pl.DeviceIdType.MESH)

    dims = (((0,), (0,)), ((), ()))
    real = imag = None
    for col in range(3):
        for q in range(2):
            for copy in loads[q * 3 + col]:
                copy.wait()
        vr, vi = vec[0, col], vec[1, col]
        pr, pi = prop[0, col], prop[1, col]
        dot = functools.partial(lax.dot_general, dimension_numbers=dims, preferred_element_type=F32)
        re = dot(pr, vr) + dot(pi, vi)
        im = dot(pi, vr) - dot(pr, vi)
        real = re if real is None else real + re
        imag = im if imag is None else imag + im
    for xx in range(X):
        xsend[xx, 0] = real[xx * wide:(xx + 1) * wide]
        xsend[xx, 1] = imag[xx * wide:(xx + 1) * wide]

    pl.semaphore_wait(barrier, len(partners))

    xcopies = []
    for d in (2, 1, 3):
        xx = lax.rem(x + d, X)
        copy = send(
            xsend.at[xx], xrecv.at[x], xs_sem.at[d], xr_sem.at[x], device(xx, y, ring, core)
        )
        copy.start()
        xcopies.append(copy)
    other = device(x, y, ring, 1 - core)
    for copy in own_items:
        copy.wait()
    items = [
        send(sink_hbm, sink.at[pl.ds(core, 1)], item_send.at[0], item_recv.at[0], other),
        send(mom_hbm, mom.at[pl.ds(core, 1)], item_send.at[1], item_recv.at[1], other),
    ]
    for copy in items:
        copy.start()
    total = xsend[x]
    for d in (1, 3, 2):
        xx = lax.rem(x + d, X)
        pltpu.make_async_copy(xrecv.at[xx], xrecv.at[xx], xr_sem.at[xx]).wait()
        total = total + xrecv[xx]
    for hh in range(2):
        zsend[hh] = total[:, hh * narrow:(hh + 1) * narrow]

    def zcopy(off, slot):
        to = lax.rem(ring + ZR - off, ZR)
        return send(
            zsend.at[lax.div(to, ZL)], zrecv.at[slot], zs_sem.at[slot], zr_sem.at[slot],
            device(x, y, to, core),
        )

    zcopies = [zcopy(off, slot) for slot, off in enumerate(OFFSETS)]
    for copy in zcopies:
        copy.start()

    @pl.when(special)
    def _():
        zcopy(4 + core, 7).start()
        zcopy(10 + core, 8).start()

    def arrived(slot):
        pltpu.make_async_copy(zrecv.at[slot], zrecv.at[slot], zr_sem.at[slot]).wait()
        return zrecv[slot]

    def ysend(src, dst, n, kind, r):
        yy = lax.rem(y + r, Y)
        return send(
            src, dst, ys_sem.at[kind, r], yr_sem.at[kind, y], device(x, yy, ring, core)
        )

    order = (4, 3, 5, 2, 6, 1, 7)
    ycopies = []
    gath[y, 0] = (arrived(2) + arrived(1)).astype(BF16)
    gath[y, 1] = (arrived(4) + arrived(3)).astype(BF16)
    for r in order:
        ycopies.append(ysend(gath.at[y, pl.ds(0, 2)], gath.at[y, pl.ds(0, 2)], 2, 0, r))
        ycopies[-1].start()
    gath[y, 3] = (arrived(6) + arrived(5)).astype(BF16)
    own = (zsend[h] + arrived(0)).astype(BF16)
    gath[y, 2] = own
    for r in order:
        yy = lax.rem(y + r, Y)
        slot = jnp.where(y >= yy, 2, 3)
        ycopies.append(ysend(gath.at[y, slot], gath.at[y, 2], 1, 1, r))
        ycopies[-1].start()

    @pl.when(special)
    def _():
        gath[y, 4] = (arrived(7) + arrived(8)).astype(BF16)

    slot = jnp.where(special, 4, jnp.where(core == 0, 3, 2))
    step = jnp.where(core == 0, Y - 1, 1)
    extra = send(
        gath.at[y, slot], gath.at[y, 3], ys_sem.at[2, 0], yr_sem.at[2, 0],
        device(x, lax.rem(y + step, Y), ring, core),
    )
    extra.start()

    elem_load.wait()
    stacked = jnp.concatenate([own[0], own[1]], axis=0)
    nt = (((1,), (1,)), ((), ()))
    for p in range(elem.shape[0]):
        by_real = lax.dot_general(stacked, elem[p, 0], nt, preferred_element_type=F32)
        by_imag = lax.dot_general(stacked, elem[p, 1], nt, preferred_element_type=F32)
        mix[core, p, 0] = (by_real[:narrow] - by_imag[narrow:]).astype(BF16)
        mix[core, p, 1] = (by_real[narrow:] + by_imag[:narrow]).astype(BF16)
    mix_copy = send(mix.at[core], mix.at[core], mix_sem.at[0], mix_sem.at[1], other)
    mix_copy.start()

    for copy in items:
        copy.wait_recv()
    mix_copy.wait_recv()
    for r in range(1, Y):
        yy = lax.rem(y + r, Y)
        both = gath.at[yy, pl.ds(0, 2)]
        pltpu.make_async_copy(both, both, yr_sem.at[0, yy]).wait()
        pltpu.make_async_copy(gath.at[yy, 2], gath.at[yy, 2], yr_sem.at[1, yy]).wait()
    extra.wait_recv()

    ranks[...] = jnp.zeros_like(ranks)
    lanes = ranks.shape[-1]
    count = sink.shape[-1]
    for kt in range(2):
        @pl.loop(0, count)
        def _(k):
            rel = sink[kt, k] + (ZL - c) * (2 * Y)
            rel = jnp.where(rel >= ZL * 2 * Y, rel - ZL * 2 * Y, rel)
            cls = rel // (2 * Y)
            rest = rel - cls * (2 * Y)
            yy = rest // 2
            kk = rest - yy * 2
            third = jnp.where(yy >= y, 0, 3)
            slot = jnp.where(cls == 1, 0, jnp.where(cls == 2, 1, jnp.where(cls == third, 2, 3)))
            g = gath[yy, slot].astype(F32)
            m = mix[kt, mom[kt, k]].astype(F32)
            keep = kk == core
            re = g[0] * m[0] + g[1] * m[1]
            im = g[0] * m[1] - g[1] * m[0]
            for o, v in ((0, re), (1, im)):
                s = v[:, :lanes]
                for part in range(1, v.shape[1] // lanes):
                    s = s + v[:, part * lanes:(part + 1) * lanes]
                s = jnp.where(keep, jnp.sum(s, axis=0, keepdims=True), 0.0)
                ranks[pl.ds((kt * 2 + o) * count + k, 1)] = s

    me = space * 2 + core
    row = lax.dot_general(
        jnp.ones((8, lanes), F32), ranks[...], nt,
        precision=lax.Precision.HIGHEST, preferred_element_type=F32,
    )
    rows[me] = row[:1]
    fcopies = []
    for n, d in enumerate(final):
        copy = send(rows.at[me], rows.at[me], fs_sem.at[n], fr_sem.at[me], final_device(*d))
        copy.start()
        fcopies.append(copy)
    for dx, dz, dk in final:
        src = lax.rem(h + dz, 2) * X + lax.rem(x + dx, X)
        src = src * 2 + ((1 - core) if dk else core)
        pltpu.make_async_copy(rows.at[src], rows.at[src], fr_sem.at[src]).wait()
    acc = rows[0]
    for n in range(1, 4 * X):
        acc = acc + rows[n]
    mine = jnp.where(core == 0, acc[:, :2 * count], acc[:, 2 * count:4 * count])
    out_ref[0:1] = mine[:, :count]
    out_ref[1:2] = mine[:, count:]

    for copy in xcopies + items + zcopies + ycopies + [extra, mix_copy] + fcopies:
        copy.wait_send()
    @pl.when(special)
    def _():
        zcopy(4 + core, 7).wait_send()
        zcopy(10 + core, 8).wait_send()


def on_device(eigvecs, propagator, elementals, sink_times, momenta):
    nvec, cols, sites = eigvecs.shape[-1], propagator.shape[-1], eigvecs.shape[3]
    nmom, items = elementals.shape[1], sink_times.shape[1]
    wide, narrow = cols // X, cols // X // 2
    dma = pltpu.SemaphoreType.DMA
    out = pl.pallas_call(
        kernel,
        out_shape=jax.ShapeDtypeStruct((2, items), F32),
        in_specs=[pl.BlockSpec(memory_space=pl.ANY)] * 5,
        out_specs=pl.BlockSpec(memory_space=pltpu.VMEM),
        scratch_shapes=[
            pltpu.VMEM((2, 3, sites, nvec), BF16),
            pltpu.VMEM((2, 3, sites, cols), BF16),
            pltpu.VMEM((nmom, 2, nvec, nvec), BF16),
            pltpu.VMEM((X, 2, wide, nvec), F32),
            pltpu.VMEM((X, 2, wide, nvec), F32),
            pltpu.VMEM((2, 2, narrow, nvec), F32),
            pltpu.VMEM((9, 2, narrow, nvec), F32),
            pltpu.VMEM((Y, 5, 2, narrow, nvec), BF16),
            pltpu.VMEM((2, nmom, 2, narrow, nvec), BF16),
            pltpu.SMEM((2, items), jnp.int32),
            pltpu.SMEM((2, items), jnp.int32),
            pltpu.VMEM((4 * X, 1, 128), F32),
            pltpu.VMEM((128, 128), F32),
            dma((2, 2, 3)), dma, dma((2,)), dma((2,)), dma((2,)),
            dma((X,)), dma((X,)), dma((9,)), dma((9,)), dma((3, Y)), dma((3, Y)),
            dma((2,)), dma((4 * X,)), dma((4 * X,)),
        ],
        compiler_params=pltpu.CompilerParams(
            collective_id=0, has_side_effects=True, vmem_limit_bytes=32 * 1024 * 1024
        ),
    )(eigvecs, propagator, elementals, sink_times, momenta)
    return out[:, None, :]


def solution(mesh):
    return jax.shard_map(
        on_device,
        mesh=mesh,
        in_specs=(
            P(None, None, "tm", "space", None),
            P(None, None, "tm", "space", None),
            P("tm", None, None, None, None),
            P("tm", None),
            P("tm", None),
        ),
        out_specs=P(None, "tm", None),
        check_vma=False,
    )
```

```python
import functools

import jax
import jax.numpy as jnp
from jax import lax
from jax.experimental import pallas as pl
from jax.experimental.pallas import tpu as pltpu
from jax.sharding import PartitionSpec as P

X, Y, ZL, CORES = 4, 8, 6, 2
ZR = 2 * ZL
OFFSETS = (6, 7, 1, 8, 2, 9, 3)
F32 = jnp.float32
BF16 = jnp.bfloat16


def kernel(
    vec_hbm, prop_hbm, elem_hbm, sink_hbm, mom_hbm, out_ref,
    vec, prop, elem, xsend, xrecv, zsend, whole, rest_send, zrecv, gath, mix, sink, mom, rows, ranks,
    load_sem, elem_sem, item_sem, item_send, item_recv,
    xs_sem, xr_sem, zs_sem, zr_sem, ys_sem, yr_sem, mix_sem, fs_sem, fr_sem,
):
    tm, space = lax.axis_index("tm"), lax.axis_index("space")
    core, chip = lax.rem(tm, 2), lax.div(tm, 2)
    y, c = lax.rem(chip, Y), lax.div(chip, Y)
    h, x = lax.div(space, X), lax.rem(space, X)
    ring = h * ZL + c
    columns = prop.shape[-1]
    wide = columns // X
    narrow = wide // 2

    def device(xx, yy, zz, kk):
        hh, cc = lax.div(zz, ZL), lax.rem(zz, ZL)
        return {"tm": (cc * Y + yy) * 2 + kk, "space": hh * X + xx}

    def send(src, dst, ssem, rsem, where):
        return pltpu.make_async_remote_copy(
            src_ref=src, dst_ref=dst, send_sem=ssem, recv_sem=rsem,
            device_id=where, device_id_type=pl.DeviceIdType.MESH,
        )

    far = lax.rem(ring + ZL, ZR)
    special = jnp.logical_or(
        jnp.logical_and(y == 0, core == 0), jnp.logical_and(y == Y - 1, core == 1)
    )
    final = [
        (dx, dz, dk) for dz in range(2) for dx in range(X) for dk in range(2) if dx or dz or dk
    ]

    def final_device(dx, dz, dk):
        return device(
            lax.rem(x + dx, X), y, far if dz else ring, (1 - core) if dk else core
        )

    loads = []
    for q in range(2):
        for col in range(3):
            a = pltpu.make_async_copy(vec_hbm.at[q, col, 0], vec.at[q, col], load_sem.at[0, q, col])
            b = pltpu.make_async_copy(prop_hbm.at[q, col, 0], prop.at[q, col], load_sem.at[1, q, col])
            a.start()
            b.start()
            loads.append((a, b))
    elem_load = pltpu.make_async_copy(elem_hbm.at[0], elem, elem_sem)
    elem_load.start()
    own_items = [
        pltpu.make_async_copy(sink_hbm, sink.at[pl.ds(core, 1)], item_sem.at[0]),
        pltpu.make_async_copy(mom_hbm, mom.at[pl.ds(core, 1)], item_sem.at[1]),
    ]
    for copy in own_items:
        copy.start()

    barrier = pltpu.get_barrier_semaphore()
    partners = [final_device(*d) for d in final]
    partners += [device(x, lax.rem(y + r, Y), ring, core) for r in range(1, Y)]
    partners += [device(x, y, lax.rem(ring + r, ZR), core) for r in range(1, ZR) if r != ZL]
    for where in partners:
        pl.semaphore_signal(barrier, inc=1, device_id=where, device_id_type=pl.DeviceIdType.MESH)

    dims = (((0,), (0,)), ((), ()))
    real = imag = None
    for col in range(3):
        for q in range(2):
            for copy in loads[q * 3 + col]:
                copy.wait()
        vr, vi = vec[0, col], vec[1, col]
        pr, pi = prop[0, col], prop[1, col]
        dot = functools.partial(lax.dot_general, dimension_numbers=dims, preferred_element_type=F32)
        re = dot(pr, vr) + dot(pi, vi)
        im = dot(pi, vr) - dot(pr, vi)
        real = re if real is None else real + re
        imag = im if imag is None else imag + im
    for xx in range(X):
        xsend[xx, 0] = real[xx * wide:(xx + 1) * wide]
        xsend[xx, 1] = imag[xx * wide:(xx + 1) * wide]

    pl.semaphore_wait(barrier, len(partners))

    xcopies = []
    for d in (2, 1, 3):
        xx = lax.rem(x + d, X)
        copy = send(
            xsend.at[xx], xrecv.at[x], xs_sem.at[d], xr_sem.at[x], device(xx, y, ring, core)
        )
        copy.start()
        xcopies.append(copy)
    other = device(x, y, ring, 1 - core)
    for copy in own_items:
        copy.wait()
    items = [
        send(sink_hbm, sink.at[pl.ds(core, 1)], item_send.at[0], item_recv.at[0], other),
        send(mom_hbm, mom.at[pl.ds(core, 1)], item_send.at[1], item_recv.at[1], other),
    ]
    for copy in items:
        copy.start()
    total = xsend[x]
    for d in (1, 3, 2):
        xx = lax.rem(x + d, X)
        pltpu.make_async_copy(xrecv.at[xx], xrecv.at[xx], xr_sem.at[xx]).wait()
        total = total + xrecv[xx]
    for hh in range(2):
        part = total[:, hh * narrow:(hh + 1) * narrow]
        zsend[hh] = part.astype(BF16)
        whole[hh] = part
    rest = whole[1 - h]
    rest_send[0] = (rest - zsend[1 - h].astype(F32)).astype(BF16)

    def zcopy(off, slot):
        to = lax.rem(ring + ZR - off, ZR)
        return send(
            zsend.at[lax.div(to, ZL)], zrecv.at[slot], zs_sem.at[slot], zr_sem.at[slot],
            device(x, y, to, core),
        )

    zcopies = [zcopy(off, slot) for slot, off in enumerate(OFFSETS)]
    zcopies.append(
        send(rest_send.at[0], zrecv.at[9], zs_sem.at[9], zr_sem.at[9], device(x, y, far, core))
    )
    for copy in zcopies:
        copy.start()

    @pl.when(special)
    def _():
        zcopy(4 + core, 7).start()
        zcopy(10 + core, 8).start()

    def arrived(slot):
        pltpu.make_async_copy(zrecv.at[slot], zrecv.at[slot], zr_sem.at[slot]).wait()
        return zrecv[slot].astype(F32)

    sent = []

    def ysend(src, dst, kind, r, origin):
        return send(
            src, dst, ys_sem.at[kind, r], yr_sem.at[kind, origin],
            device(x, lax.rem(y + r, Y), ring, core),
        )

    def third(r, slot):
        return ysend(gath.at[y, slot], gath.at[y, 2], 2, r, y)

    def direct(slot):
        for r in (2, Y - 2, 1, Y - 1):
            copy = ysend(gath.at[y, slot], gath.at[y, slot], slot, r, y)
            copy.start()
            sent.append(copy)

    def ywait(kind, slot, origin):
        ref = gath.at[origin, slot]
        pltpu.make_async_copy(ref, ref, yr_sem.at[kind, origin]).wait()

    below, above = lax.rem(y + Y - 2, Y), lax.rem(y + 2, Y)

    def forward(slot):
        ywait(slot, slot, above)
        for r, back in ((Y - 2, 4), (Y - 1, 5)):
            copy = send(
                gath.at[above, slot], gath.at[above, slot], ys_sem.at[slot, back],
                yr_sem.at[slot, above], device(x, lax.rem(y + r, Y), ring, core),
            )
            copy.start()
            sent.append(copy)
        ywait(slot, slot, below)
        copy = send(
            gath.at[below, slot], gath.at[below, slot], ys_sem.at[slot, 3],
            yr_sem.at[slot, below], device(x, lax.rem(y + 1, Y), ring, core),
        )
        copy.start()
        sent.append(copy)

    order = (4, 3, 5, 2, 6, 1, 7)
    gath[y, 3] = (arrived(6) + arrived(5)).astype(BF16)
    for r in order:
        @pl.when(lax.rem(y + r, Y) > y)
        def _():
            third(r, 3).start()
    gath[y, 1] = (arrived(4) + arrived(3)).astype(BF16)
    direct(1)
    gath[y, 0] = (arrived(2) + arrived(1)).astype(BF16)
    direct(0)
    near = whole[h] + arrived(0)
    gath[y, 2] = near.astype(BF16)
    for r in order:
        @pl.when(lax.rem(y + r, Y) < y)
        def _():
            third(r, 2).start()

    @pl.when(special)
    def _():
        gath[y, 4] = (arrived(7) + arrived(8)).astype(BF16)

    slot = jnp.where(special, 4, jnp.where(core == 0, 3, 2))
    step = jnp.where(core == 0, Y - 1, 1)
    extra = send(
        gath.at[y, slot], gath.at[y, 3], ys_sem.at[2, 0], yr_sem.at[3, 0],
        device(x, lax.rem(y + step, Y), ring, core),
    )
    extra.start()
    forward(1)
    forward(0)
    own = (near + arrived(9)).astype(BF16)

    elem_load.wait()
    stacked = jnp.concatenate([own[0], own[1]], axis=0)
    nt = (((1,), (1,)), ((), ()))
    for p in range(elem.shape[0]):
        by_real = lax.dot_general(stacked, elem[p, 0], nt, preferred_element_type=F32)
        by_imag = lax.dot_general(stacked, elem[p, 1], nt, preferred_element_type=F32)
        mix[core, p, 0] = (by_real[:narrow] - by_imag[narrow:]).astype(BF16)
        mix[core, p, 1] = (by_real[narrow:] + by_imag[:narrow]).astype(BF16)
    mix_copy = send(mix.at[core], mix.at[core], mix_sem.at[0], mix_sem.at[1], other)
    mix_copy.start()

    for copy in items:
        copy.wait_recv()
    mix_copy.wait_recv()
    for r in range(1, Y):
        yy = lax.rem(y + r, Y)
        if r not in (2, Y - 2):
            ywait(0, 0, yy)
            ywait(1, 1, yy)
        ywait(2, 2, yy)
    extra.wait_recv()

    ranks[...] = jnp.zeros_like(ranks)
    lanes = ranks.shape[-1]
    count = sink.shape[-1]
    for kt in range(2):
        @pl.loop(0, count, unroll=4)
        def _(k):
            rel = sink[kt, k] + (ZL - c) * (2 * Y)
            rel = jnp.where(rel >= ZL * 2 * Y, rel - ZL * 2 * Y, rel)
            cls = rel // (2 * Y)
            rest = rel - cls * (2 * Y)
            yy = rest // 2
            kk = rest - yy * 2
            third = jnp.where(yy >= y, 0, 3)
            slot = jnp.where(cls == 1, 0, jnp.where(cls == 2, 1, jnp.where(cls == third, 2, 3)))
            g = gath[yy, slot].astype(F32)
            m = mix[kt, mom[kt, k]].astype(F32)
            keep = kk == core
            re = g[0] * m[0] + g[1] * m[1]
            im = g[0] * m[1] - g[1] * m[0]
            for o, v in ((0, re), (1, im)):
                s = v[:, :lanes]
                for part in range(1, v.shape[1] // lanes):
                    s = s + v[:, part * lanes:(part + 1) * lanes]
                s = jnp.where(keep, jnp.sum(s, axis=0, keepdims=True), 0.0)
                ranks[pl.ds((kt * 2 + o) * count + k, 1)] = s

    me = space * 2 + core
    row = lax.dot_general(
        jnp.ones((8, lanes), F32), ranks[...], nt,
        precision=lax.Precision.HIGHEST, preferred_element_type=F32,
    )
    rows[me] = row[:1]
    fcopies = []
    for n, d in enumerate(final):
        copy = send(rows.at[me], rows.at[me], fs_sem.at[n], fr_sem.at[me], final_device(*d))
        copy.start()
        fcopies.append(copy)
    for dx, dz, dk in final:
        src = lax.rem(h + dz, 2) * X + lax.rem(x + dx, X)
        src = src * 2 + ((1 - core) if dk else core)
        pltpu.make_async_copy(rows.at[src], rows.at[src], fr_sem.at[src]).wait()
    acc = rows[0]
    for n in range(1, 4 * X):
        acc = acc + rows[n]
    mine = jnp.where(core == 0, acc[:, :2 * count], acc[:, 2 * count:4 * count])
    out_ref[0:1] = mine[:, :count]
    out_ref[1:2] = mine[:, count:]

    for copy in xcopies + items + zcopies + sent + [extra, mix_copy] + fcopies:
        copy.wait_send()
    for r in order:
        third(r, 2).wait_send()

    @pl.when(special)
    def _():
        zcopy(4 + core, 7).wait_send()
        zcopy(10 + core, 8).wait_send()


def on_device(eigvecs, propagator, elementals, sink_times, momenta):
    nvec, cols, sites = eigvecs.shape[-1], propagator.shape[-1], eigvecs.shape[3]
    nmom, items = elementals.shape[1], sink_times.shape[1]
    wide, narrow = cols // X, cols // X // 2
    dma = pltpu.SemaphoreType.DMA
    out = pl.pallas_call(
        kernel,
        out_shape=jax.ShapeDtypeStruct((2, items), F32),
        in_specs=[pl.BlockSpec(memory_space=pl.ANY)] * 5,
        out_specs=pl.BlockSpec(memory_space=pltpu.VMEM),
        scratch_shapes=[
            pltpu.VMEM((2, 3, sites, nvec), BF16),
            pltpu.VMEM((2, 3, sites, cols), BF16),
            pltpu.VMEM((nmom, 2, nvec, nvec), BF16),
            pltpu.VMEM((X, 2, wide, nvec), F32),
            pltpu.VMEM((X, 2, wide, nvec), F32),
            pltpu.VMEM((2, 2, narrow, nvec), BF16),
            pltpu.VMEM((2, 2, narrow, nvec), F32),
            pltpu.VMEM((1, 2, narrow, nvec), BF16),
            pltpu.VMEM((10, 2, narrow, nvec), BF16),
            pltpu.VMEM((Y, 5, 2, narrow, nvec), BF16),
            pltpu.VMEM((2, nmom, 2, narrow, nvec), BF16),
            pltpu.SMEM((2, items), jnp.int32),
            pltpu.SMEM((2, items), jnp.int32),
            pltpu.VMEM((4 * X, 1, 128), F32),
            pltpu.VMEM((128, 128), F32),
            dma((2, 2, 3)), dma, dma((2,)), dma((2,)), dma((2,)),
            dma((X,)), dma((X,)), dma((10,)), dma((10,)), dma((3, Y)), dma((4, Y)),
            dma((2,)), dma((4 * X,)), dma((4 * X,)),
        ],
        compiler_params=pltpu.CompilerParams(
            collective_id=0, has_side_effects=True, vmem_limit_bytes=60 * 1024 * 1024
        ),
    )(eigvecs, propagator, elementals, sink_times, momenta)
    return out[:, None, :]


def solution(mesh):
    return jax.shard_map(
        on_device,
        mesh=mesh,
        in_specs=(
            P(None, None, "tm", "space", None),
            P(None, None, "tm", "space", None),
            P("tm", None, None, None, None),
            P("tm", None),
            P("tm", None),
        ),
        out_specs=P(None, "tm", None),
        check_vma=False,
    )
```

```python
import functools

import jax
import jax.numpy as jnp
from jax import lax
from jax.experimental import pallas as pl
from jax.experimental.pallas import tpu as pltpu
from jax.sharding import PartitionSpec as P

X, Y, ZL, CORES = 4, 8, 6, 2
ZR = 2 * ZL
OFFSETS = (6, 7, 1, 8, 2, 9, 3)
F32 = jnp.float32
BF16 = jnp.bfloat16


def kernel(
    vec_hbm, prop_hbm, elem_hbm, sink_hbm, mom_hbm, out_ref,
    vec, prop, elem, xsend, xrecv, zsend, whole, rest_send, zrecv, gath, mix, sink, mom, rows, ranks,
    near_sem, load_sem, elem_sem, item_sem, item_send, item_recv,
    xs_sem, xr_sem, zs_sem, zr_sem, ys_sem, yr_sem, mix_sem, fs_sem, fr_sem,
):
    tm, space = lax.axis_index("tm"), lax.axis_index("space")
    core, chip = lax.rem(tm, 2), lax.div(tm, 2)
    y, c = lax.rem(chip, Y), lax.div(chip, Y)
    h, x = lax.div(space, X), lax.rem(space, X)
    ring = h * ZL + c
    columns = prop.shape[-1]
    wide = columns // X
    narrow = wide // 2

    def device(xx, yy, zz, kk):
        hh, cc = lax.div(zz, ZL), lax.rem(zz, ZL)
        return {"tm": (cc * Y + yy) * 2 + kk, "space": hh * X + xx}

    def send(src, dst, ssem, rsem, where):
        return pltpu.make_async_remote_copy(
            src_ref=src, dst_ref=dst, send_sem=ssem, recv_sem=rsem,
            device_id=where, device_id_type=pl.DeviceIdType.MESH,
        )

    far = lax.rem(ring + ZL, ZR)
    special = jnp.logical_or(
        jnp.logical_and(y == 0, core == 0), jnp.logical_and(y == Y - 1, core == 1)
    )
    final = [
        (dx, dz, dk) for dz in range(2) for dx in range(X) for dk in range(2) if dx or dz or dk
    ]

    def final_device(dx, dz, dk):
        return device(
            lax.rem(x + dx, X), y, far if dz else ring, (1 - core) if dk else core
        )

    loads = []
    for q in range(2):
        for col in range(3):
            a = pltpu.make_async_copy(vec_hbm.at[q, col, 0], vec.at[q, col], load_sem.at[0, q, col])
            b = pltpu.make_async_copy(prop_hbm.at[q, col, 0], prop.at[q, col], load_sem.at[1, q, col])
            a.start()
            b.start()
            loads.append((a, b))
    elem_load = pltpu.make_async_copy(elem_hbm.at[0], elem, elem_sem)
    elem_load.start()
    own_items = [
        pltpu.make_async_copy(sink_hbm, sink.at[pl.ds(core, 1)], item_sem.at[0]),
        pltpu.make_async_copy(mom_hbm, mom.at[pl.ds(core, 1)], item_sem.at[1]),
    ]
    for copy in own_items:
        copy.start()

    barrier = pltpu.get_barrier_semaphore()
    other = device(x, y, ring, 1 - core)

    def along_y(r):
        return device(x, lax.rem(y + r + Y, Y), ring, core)

    def along_z(r):
        return device(x, y, lax.rem(ring + r + ZR, ZR), core)

    def tell(sem, devices):
        for where in devices:
            pl.semaphore_signal(sem, inc=1, device_id=where, device_id_type=pl.DeviceIdType.MESH)

    partners = [device(lax.rem(x + d, X), y, ring, core) for d in range(1, X)] + [other]
    partners += [along_y(1), along_y(-1), along_z(1), along_z(-1)]
    tell(barrier, partners)

    dims = (((0,), (0,)), ((), ()))
    real = imag = None
    for col in range(3):
        for q in range(2):
            for copy in loads[q * 3 + col]:
                copy.wait()
        vr, vi = vec[0, col], vec[1, col]
        pr, pi = prop[0, col], prop[1, col]
        dot = functools.partial(lax.dot_general, dimension_numbers=dims, preferred_element_type=F32)
        re = dot(pr, vr) + dot(pi, vi)
        im = dot(pi, vr) - dot(pr, vi)
        real = re if real is None else real + re
        imag = im if imag is None else imag + im
    for xx in range(X):
        xsend[xx, 0] = real[xx * wide:(xx + 1) * wide]
        xsend[xx, 1] = imag[xx * wide:(xx + 1) * wide]

    pl.semaphore_wait(barrier, len(partners))

    xcopies = []
    for d in (2, 1, 3):
        xx = lax.rem(x + d, X)
        copy = send(
            xsend.at[xx], xrecv.at[x], xs_sem.at[d], xr_sem.at[x], device(xx, y, ring, core)
        )
        copy.start()
        xcopies.append(copy)
    tell(near_sem.at[0], [along_z(1), along_z(-1)])
    tell(near_sem.at[1], [along_y(1), along_y(-1)])
    for copy in own_items:
        copy.wait()
    items = [
        send(sink_hbm, sink.at[pl.ds(core, 1)], item_send.at[0], item_recv.at[0], other),
        send(mom_hbm, mom.at[pl.ds(core, 1)], item_send.at[1], item_recv.at[1], other),
    ]
    for copy in items:
        copy.start()
    pl.semaphore_wait(near_sem.at[0], 2)
    tell(near_sem.at[2], [along_z(2), along_z(-2)])
    pl.semaphore_wait(near_sem.at[1], 2)
    tell(near_sem.at[3], [along_y(2), along_y(-2)])
    pl.semaphore_wait(near_sem.at[2], 2)
    tell(near_sem.at[4], [along_z(2), along_z(-2)])
    total = xsend[x]
    for d in (1, 3, 2):
        xx = lax.rem(x + d, X)
        pltpu.make_async_copy(xrecv.at[xx], xrecv.at[xx], xr_sem.at[xx]).wait()
        total = total + xrecv[xx]
    for hh in range(2):
        part = total[:, hh * narrow:(hh + 1) * narrow]
        zsend[hh] = part.astype(BF16)
        whole[hh] = part
    rest = whole[1 - h]
    rest_send[0] = (rest - zsend[1 - h].astype(F32)).astype(BF16)

    def zcopy(off, slot):
        to = lax.rem(ring + ZR - off, ZR)
        return send(
            zsend.at[lax.div(to, ZL)], zrecv.at[slot], zs_sem.at[slot], zr_sem.at[slot],
            device(x, y, to, core),
        )

    zcopies = [zcopy(off, slot) for slot, off in enumerate(OFFSETS)]
    zcopies.append(
        send(rest_send.at[0], zrecv.at[9], zs_sem.at[9], zr_sem.at[9], device(x, y, far, core))
    )
    pl.semaphore_wait(near_sem.at[4], 2)
    for copy in zcopies:
        copy.start()

    @pl.when(special)
    def _():
        zcopy(4 + core, 7).start()
        zcopy(10 + core, 8).start()

    def arrived(slot):
        pltpu.make_async_copy(zrecv.at[slot], zrecv.at[slot], zr_sem.at[slot]).wait()
        return zrecv[slot].astype(F32)

    sent = []

    def ysend(src, dst, kind, r, origin):
        return send(
            src, dst, ys_sem.at[kind, r], yr_sem.at[kind, origin],
            device(x, lax.rem(y + r, Y), ring, core),
        )

    def third(r, slot):
        return ysend(gath.at[y, slot], gath.at[y, 2], 2, r, y)

    def direct(slot):
        for r in (2, Y - 2, 1, Y - 1):
            copy = ysend(gath.at[y, slot], gath.at[y, slot], slot, r, y)
            copy.start()
            sent.append(copy)

    def ywait(kind, slot, origin):
        ref = gath.at[origin, slot]
        pltpu.make_async_copy(ref, ref, yr_sem.at[kind, origin]).wait()

    below, above = lax.rem(y + Y - 2, Y), lax.rem(y + 2, Y)

    def forward(slot):
        ywait(slot, slot, above)
        for r, back in ((Y - 2, 4), (Y - 1, 5)):
            copy = send(
                gath.at[above, slot], gath.at[above, slot], ys_sem.at[slot, back],
                yr_sem.at[slot, above], device(x, lax.rem(y + r, Y), ring, core),
            )
            copy.start()
            sent.append(copy)
        ywait(slot, slot, below)
        copy = send(
            gath.at[below, slot], gath.at[below, slot], ys_sem.at[slot, 3],
            yr_sem.at[slot, below], device(x, lax.rem(y + 1, Y), ring, core),
        )
        copy.start()
        sent.append(copy)

    order = (4, 3, 5, 2, 6, 1, 7)
    gath[y, 3] = (arrived(6) + arrived(5)).astype(BF16)
    pl.semaphore_wait(near_sem.at[3], 2)
    for r in order:
        @pl.when(lax.rem(y + r, Y) > y)
        def _():
            third(r, 3).start()
    gath[y, 1] = (arrived(4) + arrived(3)).astype(BF16)
    direct(1)
    gath[y, 0] = (arrived(2) + arrived(1)).astype(BF16)
    direct(0)
    near = whole[h] + arrived(0)
    gath[y, 2] = near.astype(BF16)
    for r in order:
        @pl.when(lax.rem(y + r, Y) < y)
        def _():
            third(r, 2).start()

    @pl.when(special)
    def _():
        gath[y, 4] = (arrived(7) + arrived(8)).astype(BF16)

    slot = jnp.where(special, 4, jnp.where(core == 0, 3, 2))
    step = jnp.where(core == 0, Y - 1, 1)
    extra = send(
        gath.at[y, slot], gath.at[y, 3], ys_sem.at[2, 0], yr_sem.at[3, 0],
        device(x, lax.rem(y + step, Y), ring, core),
    )
    extra.start()
    forward(1)
    forward(0)
    own = (near + arrived(9)).astype(BF16)

    elem_load.wait()
    stacked = jnp.concatenate([own[0], own[1]], axis=0)
    nt = (((1,), (1,)), ((), ()))
    for p in range(elem.shape[0]):
        by_real = lax.dot_general(stacked, elem[p, 0], nt, preferred_element_type=F32)
        by_imag = lax.dot_general(stacked, elem[p, 1], nt, preferred_element_type=F32)
        mix[core, p, 0] = (by_real[:narrow] - by_imag[narrow:]).astype(BF16)
        mix[core, p, 1] = (by_real[narrow:] + by_imag[:narrow]).astype(BF16)
    mix_copy = send(mix.at[core], mix.at[core], mix_sem.at[0], mix_sem.at[1], other)
    mix_copy.start()

    for copy in items:
        copy.wait_recv()
    mix_copy.wait_recv()
    for r in range(1, Y):
        yy = lax.rem(y + r, Y)
        if r not in (2, Y - 2):
            ywait(0, 0, yy)
            ywait(1, 1, yy)
        ywait(2, 2, yy)
    extra.wait_recv()

    ranks[...] = jnp.zeros_like(ranks)
    lanes = ranks.shape[-1]
    count = sink.shape[-1]
    for kt in range(2):
        @pl.loop(0, count, unroll=4)
        def _(k):
            rel = sink[kt, k] + (ZL - c) * (2 * Y)
            rel = jnp.where(rel >= ZL * 2 * Y, rel - ZL * 2 * Y, rel)
            cls = rel // (2 * Y)
            rest = rel - cls * (2 * Y)
            yy = rest // 2
            kk = rest - yy * 2
            third = jnp.where(yy >= y, 0, 3)
            slot = jnp.where(cls == 1, 0, jnp.where(cls == 2, 1, jnp.where(cls == third, 2, 3)))
            g = gath[yy, slot].astype(F32)
            m = mix[kt, mom[kt, k]].astype(F32)
            keep = kk == core
            re = g[0] * m[0] + g[1] * m[1]
            im = g[0] * m[1] - g[1] * m[0]
            for o, v in ((0, re), (1, im)):
                s = v[:, :lanes]
                for part in range(1, v.shape[1] // lanes):
                    s = s + v[:, part * lanes:(part + 1) * lanes]
                s = jnp.where(keep, jnp.sum(s, axis=0, keepdims=True), 0.0)
                ranks[pl.ds((kt * 2 + o) * count + k, 1)] = s

    me = space * 2 + core
    row = lax.dot_general(
        jnp.ones((8, lanes), F32), ranks[...], nt,
        precision=lax.Precision.HIGHEST, preferred_element_type=F32,
    )
    rows[me] = row[:1]
    fcopies = []
    for n, d in enumerate(final):
        copy = send(rows.at[me], rows.at[me], fs_sem.at[n], fr_sem.at[me], final_device(*d))
        copy.start()
        fcopies.append(copy)
    for dx, dz, dk in final:
        src = lax.rem(h + dz, 2) * X + lax.rem(x + dx, X)
        src = src * 2 + ((1 - core) if dk else core)
        pltpu.make_async_copy(rows.at[src], rows.at[src], fr_sem.at[src]).wait()
    acc = rows[0]
    for n in range(1, 4 * X):
        acc = acc + rows[n]
    mine = jnp.where(core == 0, acc[:, :2 * count], acc[:, 2 * count:4 * count])
    out_ref[0:1] = mine[:, :count]
    out_ref[1:2] = mine[:, count:]

    for copy in xcopies + items + zcopies + sent + [extra, mix_copy] + fcopies:
        copy.wait_send()
    for r in order:
        third(r, 2).wait_send()

    @pl.when(special)
    def _():
        zcopy(4 + core, 7).wait_send()
        zcopy(10 + core, 8).wait_send()


def on_device(eigvecs, propagator, elementals, sink_times, momenta):
    nvec, cols, sites = eigvecs.shape[-1], propagator.shape[-1], eigvecs.shape[3]
    nmom, items = elementals.shape[1], sink_times.shape[1]
    wide, narrow = cols // X, cols // X // 2
    dma = pltpu.SemaphoreType.DMA
    out = pl.pallas_call(
        kernel,
        out_shape=jax.ShapeDtypeStruct((2, items), F32),
        in_specs=[pl.BlockSpec(memory_space=pl.ANY)] * 5,
        out_specs=pl.BlockSpec(memory_space=pltpu.VMEM),
        scratch_shapes=[
            pltpu.VMEM((2, 3, sites, nvec), BF16),
            pltpu.VMEM((2, 3, sites, cols), BF16),
            pltpu.VMEM((nmom, 2, nvec, nvec), BF16),
            pltpu.VMEM((X, 2, wide, nvec), F32),
            pltpu.VMEM((X, 2, wide, nvec), F32),
            pltpu.VMEM((2, 2, narrow, nvec), BF16),
            pltpu.VMEM((2, 2, narrow, nvec), F32),
            pltpu.VMEM((1, 2, narrow, nvec), BF16),
            pltpu.VMEM((10, 2, narrow, nvec), BF16),
            pltpu.VMEM((Y, 5, 2, narrow, nvec), BF16),
            pltpu.VMEM((2, nmom, 2, narrow, nvec), BF16),
            pltpu.SMEM((2, items), jnp.int32),
            pltpu.SMEM((2, items), jnp.int32),
            pltpu.VMEM((4 * X, 1, 128), F32),
            pltpu.VMEM((128, 128), F32),
            pltpu.SemaphoreType.REGULAR((5,)), dma((2, 2, 3)), dma, dma((2,)), dma((2,)), dma((2,)),
            dma((X,)), dma((X,)), dma((10,)), dma((10,)), dma((3, Y)), dma((4, Y)),
            dma((2,)), dma((4 * X,)), dma((4 * X,)),
        ],
        compiler_params=pltpu.CompilerParams(
            collective_id=0, has_side_effects=True, vmem_limit_bytes=60 * 1024 * 1024
        ),
    )(eigvecs, propagator, elementals, sink_times, momenta)
    return out[:, None, :]


def solution(mesh):
    return jax.shard_map(
        on_device,
        mesh=mesh,
        in_specs=(
            P(None, None, "tm", "space", None),
            P(None, None, "tm", "space", None),
            P("tm", None, None, None, None),
            P("tm", None),
            P("tm", None),
        ),
        out_specs=P(None, "tm", None),
        check_vma=False,
    )
```

```python
import functools

import jax
import jax.numpy as jnp
from jax import lax
from jax.experimental import pallas as pl
from jax.experimental.pallas import tpu as pltpu
from jax.sharding import PartitionSpec as P

X, Y, ZL, CORES = 4, 8, 6, 2
ZR = 2 * ZL
OFFSETS = (6, 7, 1, 8, 2, 9, 3)
F32 = jnp.float32
BF16 = jnp.bfloat16


def kernel(
    vec_hbm, prop_hbm, elem_hbm, sink_hbm, mom_hbm, out_ref,
    vec, prop, elem, xsend, xrecv, zsend, whole, rest_send, zrecv, gath, mix, sink, mom, rows, ranks,
    near_sem, load_sem, elem_sem, item_sem, item_send, item_recv,
    xs_sem, xr_sem, zs_sem, zr_sem, ys_sem, yr_sem, mix_sem, fs_sem, fr_sem,
):
    tm, space = lax.axis_index("tm"), lax.axis_index("space")
    core, chip = lax.rem(tm, 2), lax.div(tm, 2)
    y, c = lax.rem(chip, Y), lax.div(chip, Y)
    h, x = lax.div(space, X), lax.rem(space, X)
    ring = h * ZL + c
    columns = prop.shape[-1]
    wide = columns // X
    narrow = wide // 2

    def device(xx, yy, zz, kk):
        hh, cc = lax.div(zz, ZL), lax.rem(zz, ZL)
        return {"tm": (cc * Y + yy) * 2 + kk, "space": hh * X + xx}

    def send(src, dst, ssem, rsem, where):
        return pltpu.make_async_remote_copy(
            src_ref=src, dst_ref=dst, send_sem=ssem, recv_sem=rsem,
            device_id=where, device_id_type=pl.DeviceIdType.MESH,
        )

    far = lax.rem(ring + ZL, ZR)
    special = jnp.logical_or(
        jnp.logical_and(y == 0, core == 0), jnp.logical_and(y == Y - 1, core == 1)
    )
    final = [
        (dx, dz, dk) for dz in range(2) for dx in range(X) for dk in range(2) if dx or dz or dk
    ]

    def final_device(dx, dz, dk):
        return device(
            lax.rem(x + dx, X), y, far if dz else ring, (1 - core) if dk else core
        )

    loads = []
    for q in range(2):
        for col in range(3):
            a = pltpu.make_async_copy(vec_hbm.at[q, col, 0], vec.at[q, col], load_sem.at[0, q, col])
            b = pltpu.make_async_copy(prop_hbm.at[q, col, 0], prop.at[q, col], load_sem.at[1, q, col])
            a.start()
            b.start()
            loads.append((a, b))
    elem_load = pltpu.make_async_copy(elem_hbm.at[0], elem, elem_sem)
    elem_load.start()
    own_items = [
        pltpu.make_async_copy(sink_hbm, sink.at[pl.ds(core, 1)], item_sem.at[0]),
        pltpu.make_async_copy(mom_hbm, mom.at[pl.ds(core, 1)], item_sem.at[1]),
    ]
    for copy in own_items:
        copy.start()

    barrier = pltpu.get_barrier_semaphore()
    other = device(x, y, ring, 1 - core)

    def along_y(r):
        return device(x, lax.rem(y + r + Y, Y), ring, core)

    def along_z(r):
        return device(x, y, lax.rem(ring + r + ZR, ZR), core)

    def tell(sem, devices):
        for where in devices:
            pl.semaphore_signal(sem, inc=1, device_id=where, device_id_type=pl.DeviceIdType.MESH)

    partners = [device(lax.rem(x + d, X), y, ring, core) for d in range(1, X)] + [other]
    partners += [along_y(1), along_y(-1), along_z(1), along_z(-1)]
    tell(barrier, partners)

    dims = (((0,), (0,)), ((), ()))
    real = imag = None
    for col in range(3):
        for q in range(2):
            for copy in loads[q * 3 + col]:
                copy.wait()
        if col == 2:
            pl.semaphore_wait(barrier, len(partners))
            tell(near_sem.at[0], [along_z(1), along_z(-1)])
            tell(near_sem.at[1], [along_y(1), along_y(-1)])
        vr, vi = vec[0, col], vec[1, col]
        pr, pi = prop[0, col], prop[1, col]
        dot = functools.partial(lax.dot_general, dimension_numbers=dims, preferred_element_type=F32)
        re = dot(pr, vr) + dot(pi, vi)
        im = dot(pi, vr) - dot(pr, vi)
        real = re if real is None else real + re
        imag = im if imag is None else imag + im
    for xx in range(X):
        for hh in range(2):
            first = xx * wide + hh * narrow
            xsend[hh, xx, 0] = real[first:first + narrow]
            xsend[hh, xx, 1] = imag[first:first + narrow]


    xcopies = []
    for turn, hh in enumerate((h, 1 - h)):
        for d in (2, 1, 3):
            xx = lax.rem(x + d, X)
            copy = send(
                xsend.at[hh, xx], xrecv.at[hh, x], xs_sem.at[turn, d], xr_sem.at[turn, x],
                device(xx, y, ring, core),
            )
            copy.start()
            xcopies.append(copy)
    for copy in own_items:
        copy.wait()
    items = [
        send(sink_hbm, sink.at[pl.ds(core, 1)], item_send.at[0], item_recv.at[0], other),
        send(mom_hbm, mom.at[pl.ds(core, 1)], item_send.at[1], item_recv.at[1], other),
    ]
    for copy in items:
        copy.start()
    pl.semaphore_wait(near_sem.at[0], 2)
    tell(near_sem.at[2], [along_z(-2)])
    tell(near_sem.at[6], [along_z(2)])
    pl.semaphore_wait(near_sem.at[1], 2)
    tell(near_sem.at[3], [along_y(2), along_y(-2)])
    pl.semaphore_wait(near_sem.at[2], 1)
    tell(near_sem.at[4], [along_z(-2)])
    def summed(turn, hh):
        total = xsend[hh, x]
        for d in (1, 3, 2):
            xx = lax.rem(x + d, X)
            ref = xrecv.at[hh, xx]
            pltpu.make_async_copy(ref, ref, xr_sem.at[turn, xx]).wait()
            total = total + xrecv[hh, xx]
        zsend[hh] = total.astype(BF16)
        return total

    def zcopy(off, slot):
        to = lax.rem(ring + ZR - off, ZR)
        return send(
            zsend.at[lax.div(to, ZL)], zrecv.at[slot], zs_sem.at[slot], zr_sem.at[slot],
            device(x, y, to, core),
        )

    zcopies = [zcopy(off, slot) for slot, off in enumerate(OFFSETS)]
    zcopies.append(
        send(rest_send.at[0], zrecv.at[9], zs_sem.at[9], zr_sem.at[9], device(x, y, far, core))
    )
    def same_half(off):
        return lax.div(lax.rem(ring + ZR - off, ZR), ZL) == h

    early = ring < 3

    @pl.when(jnp.logical_not(early))
    def _():
        pl.semaphore_wait(near_sem.at[6], 1)

    whole[0] = summed(0, h)
    for n in (6, 4, 2, 3, 5):
        @pl.when(same_half(OFFSETS[n]))
        def _():
            zcopies[n].start()

    rest = summed(1, 1 - h)
    rest_send[0] = (rest - zsend[1 - h].astype(F32)).astype(BF16)
    for n in (3, 5, 4, 2):
        @pl.when(jnp.logical_not(same_half(OFFSETS[n])))
        def _():
            zcopies[n].start()

    @pl.when(jnp.logical_not(jnp.logical_or(same_half(OFFSETS[6]), early)))
    def _():
        zcopies[6].start()

    pl.semaphore_wait(near_sem.at[4], 1)
    for n in (0, 1, 7):
        zcopies[n].start()

    @pl.when(early)
    def _():
        pl.semaphore_wait(near_sem.at[6], 1)
        zcopies[6].start()

    @pl.when(special)
    def _():
        tell(near_sem.at[5], [along_z(2)])
        pl.semaphore_wait(near_sem.at[5], 1)
        zcopy(4 + core, 7).start()
        zcopy(10 + core, 8).start()

    def arrived(slot):
        pltpu.make_async_copy(zrecv.at[slot], zrecv.at[slot], zr_sem.at[slot]).wait()
        return zrecv[slot].astype(F32)

    sent = []

    def ysend(src, dst, kind, r, origin):
        return send(
            src, dst, ys_sem.at[kind, r], yr_sem.at[kind, origin],
            device(x, lax.rem(y + r, Y), ring, core),
        )

    def third(r, slot):
        return ysend(gath.at[y, slot], gath.at[y, 2], 2, r, y)

    def direct(slot):
        for r in (2, Y - 2, 1, Y - 1):
            copy = ysend(gath.at[y, slot], gath.at[y, slot], slot, r, y)
            copy.start()
            sent.append(copy)

    def ywait(kind, slot, origin):
        ref = gath.at[origin, slot]
        pltpu.make_async_copy(ref, ref, yr_sem.at[kind, origin]).wait()

    below, above = lax.rem(y + Y - 2, Y), lax.rem(y + 2, Y)

    def forward(slot):
        ywait(slot, slot, above)
        for r, back in ((Y - 2, 4), (Y - 1, 5))[slot:]:
            copy = send(
                gath.at[above, slot], gath.at[above, slot], ys_sem.at[slot, back],
                yr_sem.at[slot, above], device(x, lax.rem(y + r, Y), ring, core),
            )
            copy.start()
            sent.append(copy)
        ywait(slot, slot, below)
        for r, back in ((2, 4), (1, 3))[1 - slot:]:
            copy = send(
                gath.at[below, slot], gath.at[below, slot], ys_sem.at[slot, back],
                yr_sem.at[slot, below], device(x, lax.rem(y + r, Y), ring, core),
            )
            copy.start()
            sent.append(copy)

    order = (4, 3, 5, 2, 6, 1, 7)
    gath[y, 3] = (arrived(6) + arrived(5)).astype(BF16)
    pl.semaphore_wait(near_sem.at[3], 2)
    for r in order:
        @pl.when(lax.rem(y + r, Y) > y)
        def _():
            third(r, 3).start()
    gath[y, 1] = (arrived(4) + arrived(3)).astype(BF16)
    direct(1)
    gath[y, 0] = (arrived(2) + arrived(1)).astype(BF16)
    direct(0)
    near = whole[0] + arrived(0)
    gath[y, 2] = near.astype(BF16)
    for r in order:
        @pl.when(lax.rem(y + r, Y) < y)
        def _():
            third(r, 2).start()

    @pl.when(special)
    def _():
        gath[y, 4] = (arrived(7) + arrived(8)).astype(BF16)

    slot = jnp.where(special, 4, jnp.where(core == 0, 3, 2))
    step = jnp.where(core == 0, Y - 1, 1)
    extra = send(
        gath.at[y, slot], gath.at[y, 3], ys_sem.at[2, 0], yr_sem.at[3, 0],
        device(x, lax.rem(y + step, Y), ring, core),
    )
    extra.start()
    forward(1)
    forward(0)
    own = (near + arrived(9)).astype(BF16)

    elem_load.wait()
    stacked = jnp.concatenate([own[0], own[1]], axis=0)
    nt = (((1,), (1,)), ((), ()))
    for p in range(elem.shape[0]):
        by_real = lax.dot_general(stacked, elem[p, 0], nt, preferred_element_type=F32)
        by_imag = lax.dot_general(stacked, elem[p, 1], nt, preferred_element_type=F32)
        mix[core, p, 0] = (by_real[:narrow] - by_imag[narrow:]).astype(BF16)
        mix[core, p, 1] = (by_real[narrow:] + by_imag[:narrow]).astype(BF16)
    mix_copy = send(mix.at[core], mix.at[core], mix_sem.at[0], mix_sem.at[1], other)
    mix_copy.start()

    for copy in items:
        copy.wait_recv()
    mix_copy.wait_recv()
    for r in range(1, Y):
        yy = lax.rem(y + r, Y)
        if r not in (2, Y - 2):
            ywait(0, 0, yy)
            ywait(1, 1, yy)
        ywait(2, 2, yy)
    extra.wait_recv()

    ranks[...] = jnp.zeros_like(ranks)
    lanes = ranks.shape[-1]
    count = sink.shape[-1]
    for kt in range(2):
        @pl.loop(0, count, unroll=16)
        def _(k):
            rel = sink[kt, k] + (ZL - c) * (2 * Y)
            rel = jnp.where(rel >= ZL * 2 * Y, rel - ZL * 2 * Y, rel)
            cls = rel // (2 * Y)
            rest = rel - cls * (2 * Y)
            yy = rest // 2
            kk = rest - yy * 2
            third = jnp.where(yy >= y, 0, 3)
            slot = jnp.where(cls == 1, 0, jnp.where(cls == 2, 1, jnp.where(cls == third, 2, 3)))
            g = gath[yy, slot].astype(F32)
            m = mix[kt, mom[kt, k]].astype(F32)
            keep = kk == core
            re = g[0] * m[0] + g[1] * m[1]
            im = g[0] * m[1] - g[1] * m[0]
            for o, v in ((0, re), (1, im)):
                s = v[:, :lanes]
                for part in range(1, v.shape[1] // lanes):
                    s = s + v[:, part * lanes:(part + 1) * lanes]
                s = jnp.where(keep, jnp.sum(s, axis=0, keepdims=True), 0.0)
                ranks[pl.ds((kt * 2 + o) * count + k, 1)] = s

    me = space * 2 + core
    row = lax.dot_general(
        jnp.ones((8, lanes), F32), ranks[...], nt,
        precision=lax.Precision.HIGHEST, preferred_element_type=F32,
    )
    rows[me] = row[:1]
    fcopies = []
    for n, d in enumerate(final):
        copy = send(rows.at[me], rows.at[me], fs_sem.at[n], fr_sem.at[me], final_device(*d))
        copy.start()
        fcopies.append(copy)
    for dx, dz, dk in final:
        src = lax.rem(h + dz, 2) * X + lax.rem(x + dx, X)
        src = src * 2 + ((1 - core) if dk else core)
        pltpu.make_async_copy(rows.at[src], rows.at[src], fr_sem.at[src]).wait()
    acc = rows[0]
    for n in range(1, 4 * X):
        acc = acc + rows[n]
    mine = jnp.where(core == 0, acc[:, :2 * count], acc[:, 2 * count:4 * count])
    out_ref[0:1] = mine[:, :count]
    out_ref[1:2] = mine[:, count:]

    for copy in xcopies + items + zcopies + sent + [extra, mix_copy] + fcopies:
        copy.wait_send()
    for r in order:
        third(r, 2).wait_send()

    @pl.when(special)
    def _():
        zcopy(4 + core, 7).wait_send()
        zcopy(10 + core, 8).wait_send()


def on_device(eigvecs, propagator, elementals, sink_times, momenta):
    nvec, cols, sites = eigvecs.shape[-1], propagator.shape[-1], eigvecs.shape[3]
    nmom, items = elementals.shape[1], sink_times.shape[1]
    narrow = cols // X // 2
    dma = pltpu.SemaphoreType.DMA
    out = pl.pallas_call(
        kernel,
        out_shape=jax.ShapeDtypeStruct((2, items), F32),
        in_specs=[pl.BlockSpec(memory_space=pl.ANY)] * 5,
        out_specs=pl.BlockSpec(memory_space=pltpu.VMEM),
        scratch_shapes=[
            pltpu.VMEM((2, 3, sites, nvec), BF16),
            pltpu.VMEM((2, 3, sites, cols), BF16),
            pltpu.VMEM((nmom, 2, nvec, nvec), BF16),
            pltpu.VMEM((2, X, 2, narrow, nvec), F32),
            pltpu.VMEM((2, X, 2, narrow, nvec), F32),
            pltpu.VMEM((2, 2, narrow, nvec), BF16),
            pltpu.VMEM((1, 2, narrow, nvec), F32),
            pltpu.VMEM((1, 2, narrow, nvec), BF16),
            pltpu.VMEM((10, 2, narrow, nvec), BF16),
            pltpu.VMEM((Y, 5, 2, narrow, nvec), BF16),
            pltpu.VMEM((2, nmom, 2, narrow, nvec), BF16),
            pltpu.SMEM((2, items), jnp.int32),
            pltpu.SMEM((2, items), jnp.int32),
            pltpu.VMEM((4 * X, 1, 128), F32),
            pltpu.VMEM((128, 128), F32),
            pltpu.SemaphoreType.REGULAR((7,)), dma((2, 2, 3)), dma, dma((2,)), dma((2,)), dma((2,)),
            dma((2, X)), dma((2, X)), dma((10,)), dma((10,)), dma((3, Y)), dma((4, Y)),
            dma((2,)), dma((4 * X,)), dma((4 * X,)),
        ],
        compiler_params=pltpu.CompilerParams(
            collective_id=0, has_side_effects=True, vmem_limit_bytes=60 * 1024 * 1024
        ),
    )(eigvecs, propagator, elementals, sink_times, momenta)
    return out[:, None, :]


def solution(mesh):
    return jax.shard_map(
        on_device,
        mesh=mesh,
        in_specs=(
            P(None, None, "tm", "space", None),
            P(None, None, "tm", "space", None),
            P("tm", None, None, None, None),
            P("tm", None),
            P("tm", None),
        ),
        out_specs=P(None, "tm", None),
        check_vma=False,
    )
```

```python
import functools

import jax
import jax.numpy as jnp
from jax import lax
from jax.experimental import pallas as pl
from jax.experimental.pallas import tpu as pltpu
from jax.sharding import PartitionSpec as P

X, Y, ZL, CORES = 4, 8, 6, 2
ZR = 2 * ZL
OFFSETS = (6, 7, 1, 8, 2, 9, 3)
F32 = jnp.float32
BF16 = jnp.bfloat16


def kernel(
    vec_hbm, prop_hbm, elem_hbm, sink_hbm, mom_hbm, out_ref,
    vec, prop, elem, xsend, xrecv, zsend, whole, rest_send, zrecv, gath, mix, sink, mom, rows, ranks,
    near_sem, load_sem, elem_sem, item_sem, item_send, item_recv,
    xs_sem, xr_sem, zs_sem, zr_sem, ys_sem, yr_sem, mix_sem, fs_sem, fr_sem,
):
    tm, space = lax.axis_index("tm"), lax.axis_index("space")
    core, chip = lax.rem(tm, 2), lax.div(tm, 2)
    y, c = lax.rem(chip, Y), lax.div(chip, Y)
    h, x = lax.div(space, X), lax.rem(space, X)
    ring = h * ZL + c
    columns = prop.shape[-1]
    wide = columns // X
    narrow = wide // 2

    def device(xx, yy, zz, kk):
        hh, cc = lax.div(zz, ZL), lax.rem(zz, ZL)
        return {"tm": (cc * Y + yy) * 2 + kk, "space": hh * X + xx}

    def send(src, dst, ssem, rsem, where):
        return pltpu.make_async_remote_copy(
            src_ref=src, dst_ref=dst, send_sem=ssem, recv_sem=rsem,
            device_id=where, device_id_type=pl.DeviceIdType.MESH,
        )

    far = lax.rem(ring + ZL, ZR)
    special = jnp.logical_or(
        jnp.logical_and(y == 0, core == 0), jnp.logical_and(y == Y - 1, core == 1)
    )
    final = [
        (dx, dz, dk) for dz in range(2) for dx in range(X) for dk in range(2) if dx or dz or dk
    ]

    def final_device(dx, dz, dk):
        return device(
            lax.rem(x + dx, X), y, far if dz else ring, (1 - core) if dk else core
        )

    loads = []
    for q in range(2):
        for col in range(3):
            a = pltpu.make_async_copy(vec_hbm.at[q, col, 0], vec.at[q, col], load_sem.at[0, q, col])
            b = pltpu.make_async_copy(prop_hbm.at[q, col, 0], prop.at[q, col], load_sem.at[1, q, col])
            a.start()
            b.start()
            loads.append((a, b))
    elem_load = pltpu.make_async_copy(elem_hbm.at[0], elem, elem_sem)
    elem_load.start()
    own_items = [
        pltpu.make_async_copy(sink_hbm, sink.at[pl.ds(core, 1)], item_sem.at[0]),
        pltpu.make_async_copy(mom_hbm, mom.at[pl.ds(core, 1)], item_sem.at[1]),
    ]
    for copy in own_items:
        copy.start()

    barrier = pltpu.get_barrier_semaphore()
    other = device(x, y, ring, 1 - core)

    def along_y(r):
        return device(x, lax.rem(y + r + Y, Y), ring, core)

    def along_z(r):
        return device(x, y, lax.rem(ring + r + ZR, ZR), core)

    def tell(sem, devices):
        for where in devices:
            pl.semaphore_signal(sem, inc=1, device_id=where, device_id_type=pl.DeviceIdType.MESH)

    partners = [device(lax.rem(x + d, X), y, ring, core) for d in range(1, X)] + [other]
    partners += [along_y(1), along_y(-1), along_z(1), along_z(-1)]
    tell(barrier, partners)

    dims = (((0,), (0,)), ((), ()))
    real = imag = None
    for col in range(3):
        for q in range(2):
            for copy in loads[q * 3 + col]:
                copy.wait()
        if col == 2:
            pl.semaphore_wait(barrier, len(partners))
            tell(near_sem.at[0], [along_z(1), along_z(-1)])
            tell(near_sem.at[1], [along_y(1), along_y(-1)])
        vr, vi = vec[0, col], vec[1, col]
        pr, pi = prop[0, col], prop[1, col]
        dot = functools.partial(lax.dot_general, dimension_numbers=dims, preferred_element_type=F32)
        re = dot(pr, vr) + dot(pi, vi)
        im = dot(pi, vr) - dot(pr, vi)
        real = re if real is None else real + re
        imag = im if imag is None else imag + im
    for xx in range(X):
        for hh in range(2):
            first = xx * wide + hh * narrow
            xsend[hh, xx, 0] = real[first:first + narrow]
            xsend[hh, xx, 1] = imag[first:first + narrow]


    xcopies = []
    for turn, hh in enumerate((h, 1 - h)):
        for d in (2, 1, 3):
            xx = lax.rem(x + d, X)
            copy = send(
                xsend.at[hh, xx], xrecv.at[hh, x], xs_sem.at[turn, d], xr_sem.at[turn, x],
                device(xx, y, ring, core),
            )
            copy.start()
            xcopies.append(copy)
    for copy in own_items:
        copy.wait()
    items = [
        send(sink_hbm, sink.at[pl.ds(core, 1)], item_send.at[0], item_recv.at[0], other),
        send(mom_hbm, mom.at[pl.ds(core, 1)], item_send.at[1], item_recv.at[1], other),
    ]
    for copy in items:
        copy.start()
    pl.semaphore_wait(near_sem.at[0], 2)
    tell(near_sem.at[2], [along_z(-2)])
    tell(near_sem.at[6], [along_z(2)])
    pl.semaphore_wait(near_sem.at[1], 2)
    tell(near_sem.at[3], [along_y(2), along_y(-2)])
    pl.semaphore_wait(near_sem.at[2], 1)
    tell(near_sem.at[4], [along_z(-2)])
    def summed(turn, hh):
        total = xsend[hh, x]
        for d in (1, 3, 2):
            xx = lax.rem(x + d, X)
            ref = xrecv.at[hh, xx]
            pltpu.make_async_copy(ref, ref, xr_sem.at[turn, xx]).wait()
            total = total + xrecv[hh, xx]
        zsend[hh] = total.astype(BF16)
        return total

    def zcopy(off, slot):
        to = lax.rem(ring + ZR - off, ZR)
        return send(
            zsend.at[lax.div(to, ZL)], zrecv.at[slot], zs_sem.at[slot], zr_sem.at[slot],
            device(x, y, to, core),
        )

    zcopies = [zcopy(off, slot) for slot, off in enumerate(OFFSETS)]
    zcopies.append(
        send(rest_send.at[0], zrecv.at[9], zs_sem.at[9], zr_sem.at[9], device(x, y, far, core))
    )
    def same_half(off):
        return lax.div(lax.rem(ring + ZR - off, ZR), ZL) == h

    early = ring < 3

    @pl.when(jnp.logical_not(early))
    def _():
        pl.semaphore_wait(near_sem.at[6], 1)

    whole[0] = summed(0, h)
    for n in (6, 4, 2, 3, 5):
        @pl.when(same_half(OFFSETS[n]))
        def _():
            zcopies[n].start()

    rest = summed(1, 1 - h)
    rest_send[0] = (rest - zsend[1 - h].astype(F32)).astype(BF16)
    for n in (3, 5, 4, 2):
        @pl.when(jnp.logical_not(same_half(OFFSETS[n])))
        def _():
            zcopies[n].start()

    @pl.when(jnp.logical_not(jnp.logical_or(same_half(OFFSETS[6]), early)))
    def _():
        zcopies[6].start()

    pl.semaphore_wait(near_sem.at[4], 1)
    for n in (0, 1, 7):
        zcopies[n].start()

    @pl.when(early)
    def _():
        pl.semaphore_wait(near_sem.at[6], 1)
        zcopies[6].start()

    @pl.when(special)
    def _():
        tell(near_sem.at[5], [along_z(2)])
        pl.semaphore_wait(near_sem.at[5], 1)
        zcopy(4 + core, 7).start()
        zcopy(10 + core, 8).start()

    def arrived(slot):
        pltpu.make_async_copy(zrecv.at[slot], zrecv.at[slot], zr_sem.at[slot]).wait()
        return zrecv[slot].astype(F32)

    sent = []

    def ysend(src, dst, kind, r, origin):
        return send(
            src, dst, ys_sem.at[kind, r], yr_sem.at[kind, origin],
            device(x, lax.rem(y + r, Y), ring, core),
        )

    def third(r, slot):
        return ysend(gath.at[y, slot], gath.at[y, 2], 2, r, y)

    def direct(slot):
        for r in (2, Y - 2, 1, Y - 1):
            copy = ysend(gath.at[y, slot], gath.at[y, slot], slot, r, y)
            copy.start()
            sent.append(copy)

    def ywait(kind, slot, origin):
        ref = gath.at[origin, slot]
        pltpu.make_async_copy(ref, ref, yr_sem.at[kind, origin]).wait()

    below, above = lax.rem(y + Y - 2, Y), lax.rem(y + 2, Y)

    def forward(slot):
        ywait(slot, slot, above)
        for r, back in ((Y - 2, 4), (Y - 1, 5))[slot:]:
            copy = send(
                gath.at[above, slot], gath.at[above, slot], ys_sem.at[slot, back],
                yr_sem.at[slot, above], device(x, lax.rem(y + r, Y), ring, core),
            )
            copy.start()
            sent.append(copy)
        ywait(slot, slot, below)
        for r, back in ((2, 4), (1, 3))[1 - slot:]:
            copy = send(
                gath.at[below, slot], gath.at[below, slot], ys_sem.at[slot, back],
                yr_sem.at[slot, below], device(x, lax.rem(y + r, Y), ring, core),
            )
            copy.start()
            sent.append(copy)

    order = (4, 3, 5, 2, 6, 1, 7)
    pl.semaphore_wait(near_sem.at[3], 2)
    gath[y, 1] = (arrived(4) + arrived(3)).astype(BF16)
    direct(1)
    gath[y, 0] = (arrived(2) + arrived(1)).astype(BF16)
    direct(0)
    gath[y, 3] = (arrived(6) + arrived(5)).astype(BF16)
    for r in order:
        @pl.when(lax.rem(y + r, Y) > y)
        def _():
            third(r, 3).start()
    near = whole[0] + arrived(0)
    gath[y, 2] = near.astype(BF16)
    for r in order:
        @pl.when(lax.rem(y + r, Y) < y)
        def _():
            third(r, 2).start()
    @pl.when(special)
    def _():
        gath[y, 4] = (arrived(7) + arrived(8)).astype(BF16)

    slot = jnp.where(special, 4, jnp.where(core == 0, 3, 2))
    step = jnp.where(core == 0, Y - 1, 1)
    extra = send(
        gath.at[y, slot], gath.at[y, 3], ys_sem.at[2, 0], yr_sem.at[3, 0],
        device(x, lax.rem(y + step, Y), ring, core),
    )
    extra.start()
    forward(1)
    forward(0)
    own = (near + arrived(9)).astype(BF16)

    elem_load.wait()
    stacked = jnp.concatenate([own[0], own[1]], axis=0)
    nt = (((1,), (1,)), ((), ()))
    for p in range(elem.shape[0]):
        by_real = lax.dot_general(stacked, elem[p, 0], nt, preferred_element_type=F32)
        by_imag = lax.dot_general(stacked, elem[p, 1], nt, preferred_element_type=F32)
        mix[core, p, 0] = (by_real[:narrow] - by_imag[narrow:]).astype(BF16)
        mix[core, p, 1] = (by_real[narrow:] + by_imag[:narrow]).astype(BF16)
    mix_copy = send(mix.at[core], mix.at[core], mix_sem.at[0], mix_sem.at[1], other)
    mix_copy.start()

    for copy in items:
        copy.wait_recv()
    mix_copy.wait_recv()
    for r in range(1, Y):
        yy = lax.rem(y + r, Y)
        if r not in (2, Y - 2):
            ywait(0, 0, yy)
            ywait(1, 1, yy)
        ywait(2, 2, yy)
    extra.wait_recv()

    ranks[...] = jnp.zeros_like(ranks)
    lanes = ranks.shape[-1]
    count = sink.shape[-1]
    for kt in range(2):
        @pl.loop(0, count, unroll=16)
        def _(k):
            rel = sink[kt, k] + (ZL - c) * (2 * Y)
            rel = jnp.where(rel >= ZL * 2 * Y, rel - ZL * 2 * Y, rel)
            cls = rel // (2 * Y)
            rest = rel - cls * (2 * Y)
            yy = rest // 2
            kk = rest - yy * 2
            third = jnp.where(yy >= y, 0, 3)
            slot = jnp.where(cls == 1, 0, jnp.where(cls == 2, 1, jnp.where(cls == third, 2, 3)))
            g = gath[yy, slot].astype(F32)
            m = mix[kt, mom[kt, k]].astype(F32)
            keep = kk == core
            re = g[0] * m[0] + g[1] * m[1]
            im = g[0] * m[1] - g[1] * m[0]
            for o, v in ((0, re), (1, im)):
                s = v[:, :lanes]
                for part in range(1, v.shape[1] // lanes):
                    s = s + v[:, part * lanes:(part + 1) * lanes]
                s = jnp.where(keep, jnp.sum(s, axis=0, keepdims=True), 0.0)
                ranks[pl.ds((kt * 2 + o) * count + k, 1)] = s

    me = space * 2 + core
    row = lax.dot_general(
        jnp.ones((8, lanes), F32), ranks[...], nt,
        precision=lax.Precision.HIGHEST, preferred_element_type=F32,
    )
    rows[me] = row[:1]
    fcopies = []
    for n, d in enumerate(final):
        copy = send(rows.at[me], rows.at[me], fs_sem.at[n], fr_sem.at[me], final_device(*d))
        copy.start()
        fcopies.append(copy)
    for dx, dz, dk in final:
        src = lax.rem(h + dz, 2) * X + lax.rem(x + dx, X)
        src = src * 2 + ((1 - core) if dk else core)
        pltpu.make_async_copy(rows.at[src], rows.at[src], fr_sem.at[src]).wait()
    acc = rows[0]
    for n in range(1, 4 * X):
        acc = acc + rows[n]
    mine = jnp.where(core == 0, acc[:, :2 * count], acc[:, 2 * count:4 * count])
    out_ref[0:1] = mine[:, :count]
    out_ref[1:2] = mine[:, count:]

    for copy in xcopies + items + zcopies + sent + [extra, mix_copy] + fcopies:
        copy.wait_send()
    for r in order:
        third(r, 2).wait_send()

    @pl.when(special)
    def _():
        zcopy(4 + core, 7).wait_send()
        zcopy(10 + core, 8).wait_send()


def on_device(eigvecs, propagator, elementals, sink_times, momenta):
    nvec, cols, sites = eigvecs.shape[-1], propagator.shape[-1], eigvecs.shape[3]
    nmom, items = elementals.shape[1], sink_times.shape[1]
    narrow = cols // X // 2
    dma = pltpu.SemaphoreType.DMA
    out = pl.pallas_call(
        kernel,
        out_shape=jax.ShapeDtypeStruct((2, items), F32),
        in_specs=[pl.BlockSpec(memory_space=pl.ANY)] * 5,
        out_specs=pl.BlockSpec(memory_space=pltpu.VMEM),
        scratch_shapes=[
            pltpu.VMEM((2, 3, sites, nvec), BF16),
            pltpu.VMEM((2, 3, sites, cols), BF16),
            pltpu.VMEM((nmom, 2, nvec, nvec), BF16),
            pltpu.VMEM((2, X, 2, narrow, nvec), F32),
            pltpu.VMEM((2, X, 2, narrow, nvec), F32),
            pltpu.VMEM((2, 2, narrow, nvec), BF16),
            pltpu.VMEM((1, 2, narrow, nvec), F32),
            pltpu.VMEM((1, 2, narrow, nvec), BF16),
            pltpu.VMEM((10, 2, narrow, nvec), BF16),
            pltpu.VMEM((Y, 5, 2, narrow, nvec), BF16),
            pltpu.VMEM((2, nmom, 2, narrow, nvec), BF16),
            pltpu.SMEM((2, items), jnp.int32),
            pltpu.SMEM((2, items), jnp.int32),
            pltpu.VMEM((4 * X, 1, 128), F32),
            pltpu.VMEM((128, 128), F32),
            pltpu.SemaphoreType.REGULAR((7,)), dma((2, 2, 3)), dma, dma((2,)), dma((2,)), dma((2,)),
            dma((2, X)), dma((2, X)), dma((10,)), dma((10,)), dma((3, Y)), dma((4, Y)),
            dma((2,)), dma((4 * X,)), dma((4 * X,)),
        ],
        compiler_params=pltpu.CompilerParams(
            collective_id=0, has_side_effects=True, vmem_limit_bytes=60 * 1024 * 1024
        ),
    )(eigvecs, propagator, elementals, sink_times, momenta)
    return out[:, None, :]


def solution(mesh):
    return jax.shard_map(
        on_device,
        mesh=mesh,
        in_specs=(
            P(None, None, "tm", "space", None),
            P(None, None, "tm", "space", None),
            P("tm", None, None, None, None),
            P("tm", None),
            P("tm", None),
        ),
        out_specs=P(None, "tm", None),
        check_vma=False,
    )
```

```python
import functools

import jax
import jax.numpy as jnp
from jax import lax
from jax.experimental import pallas as pl
from jax.experimental.pallas import tpu as pltpu
from jax.sharding import PartitionSpec as P

X, Y, ZL, CORES = 4, 8, 6, 2
ZR = 2 * ZL
OFFSETS = (6, 7, 1, 8, 2, 9, 3)
F32 = jnp.float32
BF16 = jnp.bfloat16


def kernel(
    vec_hbm, prop_hbm, elem_hbm, sink_hbm, mom_hbm, out_ref,
    vec, prop, elem, xsend, xrecv, zsend, whole, rest_send, zrecv, gath, mix, sink, mom, rows, ranks,
    near_sem, load_sem, elem_sem, item_sem, item_send, item_recv,
    xs_sem, xr_sem, zs_sem, zr_sem, ys_sem, yr_sem, mix_sem, fs_sem, fr_sem,
):
    tm, space = lax.axis_index("tm"), lax.axis_index("space")
    core, chip = lax.rem(tm, 2), lax.div(tm, 2)
    y, c = lax.rem(chip, Y), lax.div(chip, Y)
    h, x = lax.div(space, X), lax.rem(space, X)
    ring = h * ZL + c
    columns = prop.shape[-1]
    wide = columns // X
    narrow = wide // 2

    def device(xx, yy, zz, kk):
        hh, cc = lax.div(zz, ZL), lax.rem(zz, ZL)
        return {"tm": (cc * Y + yy) * 2 + kk, "space": hh * X + xx}

    def send(src, dst, ssem, rsem, where):
        return pltpu.make_async_remote_copy(
            src_ref=src, dst_ref=dst, send_sem=ssem, recv_sem=rsem,
            device_id=where, device_id_type=pl.DeviceIdType.MESH,
        )

    far = lax.rem(ring + ZL, ZR)
    special = jnp.logical_or(
        jnp.logical_and(y == 0, core == 0), jnp.logical_and(y == Y - 1, core == 1)
    )
    final = [
        (dx, dz, dk) for dz in (1, 0) for dx in (2, 1, 3, 0) for dk in range(2) if dx or dz or dk
    ]

    def final_device(dx, dz, dk):
        return device(
            lax.rem(x + dx, X), y, far if dz else ring, (1 - core) if dk else core
        )

    loads = []
    for q in range(2):
        for col in range(3):
            a = pltpu.make_async_copy(vec_hbm.at[q, col, 0], vec.at[q, col], load_sem.at[0, q, col])
            b = pltpu.make_async_copy(prop_hbm.at[q, col, 0], prop.at[q, col], load_sem.at[1, q, col])
            a.start()
            b.start()
            loads.append((a, b))
    elem_load = pltpu.make_async_copy(elem_hbm.at[0], elem, elem_sem)
    elem_load.start()
    own_items = [
        pltpu.make_async_copy(sink_hbm, sink.at[pl.ds(core, 1)], item_sem.at[0]),
        pltpu.make_async_copy(mom_hbm, mom.at[pl.ds(core, 1)], item_sem.at[1]),
    ]
    for copy in own_items:
        copy.start()

    barrier = pltpu.get_barrier_semaphore()
    other = device(x, y, ring, 1 - core)

    def along_y(r):
        return device(x, lax.rem(y + r + Y, Y), ring, core)

    def along_z(r):
        return device(x, y, lax.rem(ring + r + ZR, ZR), core)

    def tell(sem, devices):
        for where in devices:
            pl.semaphore_signal(sem, inc=1, device_id=where, device_id_type=pl.DeviceIdType.MESH)

    partners = [device(lax.rem(x + d, X), y, ring, core) for d in range(1, X)] + [other]
    partners += [along_y(1), along_y(-1), along_z(1), along_z(-1)]
    tell(barrier, partners)

    dims = (((0,), (0,)), ((), ()))
    real = imag = None
    for col in range(3):
        for q in range(2):
            for copy in loads[q * 3 + col]:
                copy.wait()
        if col == 2:
            pl.semaphore_wait(barrier, len(partners))
            tell(near_sem.at[0], [along_z(1), along_z(-1)])
            tell(near_sem.at[1], [along_y(1), along_y(-1)])
        vr, vi = vec[0, col], vec[1, col]
        pr, pi = prop[0, col], prop[1, col]
        dot = functools.partial(lax.dot_general, dimension_numbers=dims, preferred_element_type=F32)
        re = dot(pr, vr) + dot(pi, vi)
        im = dot(pi, vr) - dot(pr, vi)
        real = re if real is None else real + re
        imag = im if imag is None else imag + im
    for xx in range(X):
        for hh in range(2):
            first = xx * wide + hh * narrow
            xsend[hh, xx, 0] = real[first:first + narrow]
            xsend[hh, xx, 1] = imag[first:first + narrow]


    xcopies = []
    for turn, hh in enumerate((h, 1 - h)):
        for d in (2, 1, 3):
            xx = lax.rem(x + d, X)
            copy = send(
                xsend.at[hh, xx], xrecv.at[hh, x], xs_sem.at[turn, d], xr_sem.at[turn, x],
                device(xx, y, ring, core),
            )
            copy.start()
            xcopies.append(copy)
    for copy in own_items:
        copy.wait()
    items = [
        send(sink_hbm, sink.at[pl.ds(core, 1)], item_send.at[0], item_recv.at[0], other),
        send(mom_hbm, mom.at[pl.ds(core, 1)], item_send.at[1], item_recv.at[1], other),
    ]
    for copy in items:
        copy.start()
    pl.semaphore_wait(near_sem.at[0], 2)
    tell(near_sem.at[2], [along_z(-2)])
    tell(near_sem.at[6], [along_z(2)])
    pl.semaphore_wait(near_sem.at[1], 2)
    tell(near_sem.at[3], [along_y(2), along_y(-2)])
    pl.semaphore_wait(near_sem.at[2], 1)
    tell(near_sem.at[4], [along_z(-2)])
    def summed(turn, hh):
        total = xsend[hh, x]
        for d in (1, 3, 2):
            xx = lax.rem(x + d, X)
            ref = xrecv.at[hh, xx]
            pltpu.make_async_copy(ref, ref, xr_sem.at[turn, xx]).wait()
            total = total + xrecv[hh, xx]
        zsend[hh] = total.astype(BF16)
        return total

    def zcopy(off, slot):
        to = lax.rem(ring + ZR - off, ZR)
        return send(
            zsend.at[lax.div(to, ZL)], zrecv.at[slot], zs_sem.at[slot], zr_sem.at[slot],
            device(x, y, to, core),
        )

    zcopies = [zcopy(off, slot) for slot, off in enumerate(OFFSETS)]
    zcopies.append(
        send(rest_send.at[0], zrecv.at[9], zs_sem.at[9], zr_sem.at[9], device(x, y, far, core))
    )
    def same_half(off):
        return lax.div(lax.rem(ring + ZR - off, ZR), ZL) == h

    early = ring < 3

    @pl.when(jnp.logical_not(early))
    def _():
        pl.semaphore_wait(near_sem.at[6], 1)

    whole[0] = summed(0, h)
    for n in (6, 4, 2, 3, 5):
        @pl.when(same_half(OFFSETS[n]))
        def _():
            zcopies[n].start()

    rest = summed(1, 1 - h)
    rest_send[0] = (rest - zsend[1 - h].astype(F32)).astype(BF16)
    for n in (3, 5, 4, 2):
        @pl.when(jnp.logical_not(same_half(OFFSETS[n])))
        def _():
            zcopies[n].start()

    @pl.when(jnp.logical_not(jnp.logical_or(same_half(OFFSETS[6]), early)))
    def _():
        zcopies[6].start()

    pl.semaphore_wait(near_sem.at[4], 1)
    for n in (0, 1, 7):
        zcopies[n].start()

    @pl.when(early)
    def _():
        pl.semaphore_wait(near_sem.at[6], 1)
        zcopies[6].start()

    @pl.when(special)
    def _():
        tell(near_sem.at[5], [along_z(2)])
        pl.semaphore_wait(near_sem.at[5], 1)
        zcopy(4 + core, 7).start()
        zcopy(10 + core, 8).start()

    def arrived(slot):
        pltpu.make_async_copy(zrecv.at[slot], zrecv.at[slot], zr_sem.at[slot]).wait()
        return zrecv[slot].astype(F32)

    sent = []

    def ysend(src, dst, kind, r, origin):
        return send(
            src, dst, ys_sem.at[kind, r], yr_sem.at[kind, origin],
            device(x, lax.rem(y + r, Y), ring, core),
        )

    def third(r, slot):
        return ysend(gath.at[y, slot], gath.at[y, 2], 2, r, y)

    def direct(slot):
        for r in (2, Y - 2, 1, Y - 1):
            copy = ysend(gath.at[y, slot], gath.at[y, slot], slot, r, y)
            copy.start()
            sent.append(copy)

    def ywait(kind, slot, origin):
        ref = gath.at[origin, slot]
        pltpu.make_async_copy(ref, ref, yr_sem.at[kind, origin]).wait()

    below, above = lax.rem(y + Y - 2, Y), lax.rem(y + 2, Y)

    def forward(slot):
        ywait(slot, slot, above)
        for r, back in ((Y - 2, 4), (Y - 1, 5))[slot:]:
            copy = send(
                gath.at[above, slot], gath.at[above, slot], ys_sem.at[slot, back],
                yr_sem.at[slot, above], device(x, lax.rem(y + r, Y), ring, core),
            )
            copy.start()
            sent.append(copy)
        ywait(slot, slot, below)
        for r, back in ((2, 4), (1, 3))[1 - slot:]:
            copy = send(
                gath.at[below, slot], gath.at[below, slot], ys_sem.at[slot, back],
                yr_sem.at[slot, below], device(x, lax.rem(y + r, Y), ring, core),
            )
            copy.start()
            sent.append(copy)

    order = (1, 7, 2, 6, 3, 5, 4)
    pl.semaphore_wait(near_sem.at[3], 2)
    gath[y, 1] = (arrived(4) + arrived(3)).astype(BF16)
    direct(1)
    gath[y, 0] = (arrived(2) + arrived(1)).astype(BF16)
    direct(0)
    gath[y, 3] = (arrived(6) + arrived(5)).astype(BF16)
    for r in order:
        @pl.when(lax.rem(y + r, Y) > y)
        def _():
            third(r, 3).start()
    near = whole[0] + arrived(0)
    gath[y, 2] = near.astype(BF16)
    for r in order:
        @pl.when(lax.rem(y + r, Y) < y)
        def _():
            third(r, 2).start()
    @pl.when(special)
    def _():
        gath[y, 4] = (arrived(7) + arrived(8)).astype(BF16)

    slot = jnp.where(special, 4, jnp.where(core == 0, 3, 2))
    step = jnp.where(core == 0, Y - 1, 1)
    extra = send(
        gath.at[y, slot], gath.at[y, 3], ys_sem.at[2, 0], yr_sem.at[3, 0],
        device(x, lax.rem(y + step, Y), ring, core),
    )
    extra.start()
    forward(1)
    forward(0)
    own = (near + arrived(9)).astype(BF16)

    elem_load.wait()
    stacked = jnp.concatenate([own[0], own[1]], axis=0)
    nt = (((1,), (1,)), ((), ()))
    for p in range(elem.shape[0]):
        by_real = lax.dot_general(stacked, elem[p, 0], nt, preferred_element_type=F32)
        by_imag = lax.dot_general(stacked, elem[p, 1], nt, preferred_element_type=F32)
        mix[core, p, 0] = (by_real[:narrow] - by_imag[narrow:]).astype(BF16)
        mix[core, p, 1] = (by_real[narrow:] + by_imag[:narrow]).astype(BF16)
    mix_copy = send(mix.at[core], mix.at[core], mix_sem.at[0], mix_sem.at[1], other)
    mix_copy.start()

    for copy in items:
        copy.wait_recv()
    mix_copy.wait_recv()
    for r in range(1, Y):
        yy = lax.rem(y + r, Y)
        if r not in (2, Y - 2):
            ywait(0, 0, yy)
            ywait(1, 1, yy)
        ywait(2, 2, yy)
    extra.wait_recv()

    ranks[...] = jnp.zeros_like(ranks)
    lanes = ranks.shape[-1]
    count = sink.shape[-1]
    for kt in range(2):
        @pl.loop(0, count, unroll=16)
        def _(k):
            rel = sink[kt, k] + (ZL - c) * (2 * Y)
            rel = jnp.where(rel >= ZL * 2 * Y, rel - ZL * 2 * Y, rel)
            cls = rel // (2 * Y)
            rest = rel - cls * (2 * Y)
            yy = rest // 2
            kk = rest - yy * 2
            third = jnp.where(yy >= y, 0, 3)
            slot = jnp.where(cls == 1, 0, jnp.where(cls == 2, 1, jnp.where(cls == third, 2, 3)))
            g = gath[yy, slot].astype(F32)
            m = mix[kt, mom[kt, k]].astype(F32)
            keep = kk == core
            re = g[0] * m[0] + g[1] * m[1]
            im = g[0] * m[1] - g[1] * m[0]
            for o, v in ((0, re), (1, im)):
                s = v[:, :lanes]
                for part in range(1, v.shape[1] // lanes):
                    s = s + v[:, part * lanes:(part + 1) * lanes]
                s = jnp.where(keep, jnp.sum(s, axis=0, keepdims=True), 0.0)
                ranks[pl.ds((kt * 2 + o) * count + k, 1)] = s

    me = space * 2 + core
    row = lax.dot_general(
        jnp.ones((8, lanes), F32), ranks[...], nt,
        precision=lax.Precision.HIGHEST, preferred_element_type=F32,
    )
    rows[me] = row[:1]
    fcopies = []
    for n, d in enumerate(final):
        copy = send(rows.at[me], rows.at[me], fs_sem.at[n], fr_sem.at[me], final_device(*d))
        copy.start()
        fcopies.append(copy)
    for dx, dz, dk in final:
        src = lax.rem(h + dz, 2) * X + lax.rem(x + dx, X)
        src = src * 2 + ((1 - core) if dk else core)
        pltpu.make_async_copy(rows.at[src], rows.at[src], fr_sem.at[src]).wait()
    acc = rows[0]
    for n in range(1, 4 * X):
        acc = acc + rows[n]
    mine = jnp.where(core == 0, acc[:, :2 * count], acc[:, 2 * count:4 * count])
    out_ref[0:1] = mine[:, :count]
    out_ref[1:2] = mine[:, count:]

    for copy in xcopies + items + zcopies + sent + [extra, mix_copy] + fcopies:
        copy.wait_send()
    for r in order:
        third(r, 2).wait_send()

    @pl.when(special)
    def _():
        zcopy(4 + core, 7).wait_send()
        zcopy(10 + core, 8).wait_send()


def on_device(eigvecs, propagator, elementals, sink_times, momenta):
    nvec, cols, sites = eigvecs.shape[-1], propagator.shape[-1], eigvecs.shape[3]
    nmom, items = elementals.shape[1], sink_times.shape[1]
    narrow = cols // X // 2
    dma = pltpu.SemaphoreType.DMA
    out = pl.pallas_call(
        kernel,
        out_shape=jax.ShapeDtypeStruct((2, items), F32),
        in_specs=[pl.BlockSpec(memory_space=pl.ANY)] * 5,
        out_specs=pl.BlockSpec(memory_space=pltpu.VMEM),
        scratch_shapes=[
            pltpu.VMEM((2, 3, sites, nvec), BF16),
            pltpu.VMEM((2, 3, sites, cols), BF16),
            pltpu.VMEM((nmom, 2, nvec, nvec), BF16),
            pltpu.VMEM((2, X, 2, narrow, nvec), F32),
            pltpu.VMEM((2, X, 2, narrow, nvec), F32),
            pltpu.VMEM((2, 2, narrow, nvec), BF16),
            pltpu.VMEM((1, 2, narrow, nvec), F32),
            pltpu.VMEM((1, 2, narrow, nvec), BF16),
            pltpu.VMEM((10, 2, narrow, nvec), BF16),
            pltpu.VMEM((Y, 5, 2, narrow, nvec), BF16),
            pltpu.VMEM((2, nmom, 2, narrow, nvec), BF16),
            pltpu.SMEM((2, items), jnp.int32),
            pltpu.SMEM((2, items), jnp.int32),
            pltpu.VMEM((4 * X, 1, 128), F32),
            pltpu.VMEM((128, 128), F32),
            pltpu.SemaphoreType.REGULAR((7,)), dma((2, 2, 3)), dma, dma((2,)), dma((2,)), dma((2,)),
            dma((2, X)), dma((2, X)), dma((10,)), dma((10,)), dma((3, Y)), dma((4, Y)),
            dma((2,)), dma((4 * X,)), dma((4 * X,)),
        ],
        compiler_params=pltpu.CompilerParams(
            collective_id=0, has_side_effects=True, vmem_limit_bytes=60 * 1024 * 1024
        ),
    )(eigvecs, propagator, elementals, sink_times, momenta)
    return out[:, None, :]


def solution(mesh):
    return jax.shard_map(
        on_device,
        mesh=mesh,
        in_specs=(
            P(None, None, "tm", "space", None),
            P(None, None, "tm", "space", None),
            P("tm", None, None, None, None),
            P("tm", None),
            P("tm", None),
        ),
        out_specs=P(None, "tm", None),
        check_vma=False,
    )
```
